128 devices in a mesh: req: 32 (over x, y, core), head: 4 (over z).
Axes of the slice: x: 4, y: 4, z: 4, core: 2. Of those that a mesh axis runs over, the one named last changes fastest.
Arguments:
- prefill_query: bfloat16 [16384, 2048], P('req', 'head'), may hold values from -16 to 16
- prefill_new_pairs: bfloat16 [16384, 2, 1024], P('req', None, 'head'), may hold values from -16 to 16
- prefill_cache: bfloat16 [32, 2, 2048, 1024], P('req', None, None, 'head'), may hold values from -16 to 16
- prefill_start: int32 [32], P('req'), may hold values from 0 to 2048, as said below
- decode_query: bfloat16 [96, 2048], P('req', 'head'), may hold values from -16 to 16
- decode_fresh: bfloat16 [96, 2, 1024], P('req', None, 'head'), may hold values from -16 to 16
- decode_cache: bfloat16 [96, 2, 2048, 1024], P('req', None, None, 'head'), may hold values from -16 to 16
- decode_length: int32 [96], P('req'), may hold values from 2 to 2048
- decode_slot: int32 [96], P('req'), may hold values from 0 to 95, each once
- prefill_states: bfloat16 [16384, 2048], P('req', 'head'), may hold values from -32 to 32
- decode_states: bfloat16 [96, 2048], P('req', 'head'), may hold values from -32 to 32
- output_proj: bfloat16 [2048, 2048], P('head', 'req'), may hold values from -0.125 to 0.125
- norm_gain: bfloat16 [2048], replicated, may hold values from 0.099609375 to 1.8984375
- gate_weight: bfloat16 [2048, 6144], P('req', 'head'), may hold values from -0.125 to 0.125
- up_weight: bfloat16 [2048, 6144], P('req', 'head'), may hold values from -0.125 to 0.125
- down_weight: bfloat16 [6144, 2048], P('head', 'req'), may hold values from -0.078125 to 0.078125
Outputs:
- prefill_result: bfloat16 [16384, 2048], P('req', 'head')
- decode_result: bfloat16 [96, 2048], P('req', 'head')
The draws below stay inside these ranges and needn't reach their ends.
Inputs may be any that keep to these rules, and one draw needn't show every extreme that they name: `decode_slot`: a permutation; the cache of slot s is held by req index s // 3. `prefill_start`: a multiple of 512.
All inputs are finite; a program needn't handle non-finite values.
Results may differ from the reference program's by a relative error of at most 0.0094.
Values may be sent and summed in bfloat16 or wider, within the bound.
No kernel may reach another device: no remote copies, remote signals or barrier semaphores. Data moves between devices by JAX's collectives and lax.ppermute only.
A program may use at most 128 MiB of HBM per device.

```python
import math
import jax
import jax.numpy as jnp
from jax import lax

D = 2048
HQ = 16
KEY_VALUE_HEADS = 8
HEAD_SIZE = 128
FF = 6144
REQUEST_TOKENS = 512
CACHE_POSITIONS = 2048
PREFILL_REQUESTS = 32
DECODE_REQUESTS = 96
PREFILL_TOKENS = 16384


def normal_base(key, target_dims):
    return jax.random.truncated_normal(key, -4.0, 4.0, target_dims, jnp.float32)


def draw_prefill_query(key, part):
    target_dims = (PREFILL_TOKENS, HQ, HEAD_SIZE)
    base_draw = normal_base(key, target_dims)
    return base_draw.reshape(PREFILL_TOKENS, HQ * HEAD_SIZE).astype(jnp.bfloat16)


def draw_decode_query(key, part):
    target_dims = (DECODE_REQUESTS, HQ, HEAD_SIZE)
    base_draw = normal_base(key, target_dims)
    return base_draw.reshape(DECODE_REQUESTS, HQ * HEAD_SIZE).astype(jnp.bfloat16)


def draw_prefill_new_pairs(key, part):
    target_dims = (PREFILL_TOKENS, KEY_VALUE_HEADS, HEAD_SIZE)
    key_part = normal_base(jax.random.fold_in(key, 1), target_dims)
    value_part = 4.0 * normal_base(jax.random.fold_in(key, 2), target_dims)
    combined_rows = jnp.stack([key_part, value_part], axis=1)
    return combined_rows.reshape(PREFILL_TOKENS, 2, KEY_VALUE_HEADS * HEAD_SIZE).astype(jnp.bfloat16)


def draw_decode_fresh(key, part):
    target_dims = (DECODE_REQUESTS, KEY_VALUE_HEADS, HEAD_SIZE)
    key_part = normal_base(jax.random.fold_in(key, 1), target_dims)
    value_part = 4.0 * normal_base(jax.random.fold_in(key, 2), target_dims)
    combined_rows = jnp.stack([key_part, value_part], axis=1)
    return combined_rows.reshape(DECODE_REQUESTS, 2, KEY_VALUE_HEADS * HEAD_SIZE).astype(jnp.bfloat16)


def cache_draw(key, request_count_all):
    target_dims = (request_count_all, CACHE_POSITIONS, KEY_VALUE_HEADS, HEAD_SIZE)
    key_part = normal_base(jax.random.fold_in(key, 1), target_dims)
    value_part = 4.0 * normal_base(jax.random.fold_in(key, 2), target_dims)
    combined_rows = jnp.stack([key_part, value_part], axis=1)
    return combined_rows.reshape(request_count_all, 2, CACHE_POSITIONS, KEY_VALUE_HEADS * HEAD_SIZE).astype(jnp.bfloat16)


def draw_prefill_cache(key, part):
    return cache_draw(key, PREFILL_REQUESTS)


def draw_decode_cache(key, part):
    return cache_draw(key, DECODE_REQUESTS)


def draw_decode_length(key, part):
    lengths = jax.random.randint(key, (DECODE_REQUESTS,), 2, CACHE_POSITIONS + 1, dtype=jnp.int32)
    longest = jax.random.randint(jax.random.fold_in(key, 1), (), 0, DECODE_REQUESTS, dtype=jnp.int32)
    return jnp.where(jnp.arange(DECODE_REQUESTS, dtype=jnp.int32) == longest, CACHE_POSITIONS, lengths).astype(jnp.int32)


def draw_prefill_start(key, part):
    step_count = jax.random.randint(key, (PREFILL_REQUESTS,), 0, CACHE_POSITIONS // REQUEST_TOKENS + 1, dtype=jnp.int32)
    longest = jax.random.randint(jax.random.fold_in(key, 1), (), 0, PREFILL_REQUESTS, dtype=jnp.int32)
    step_count = jnp.where(jnp.arange(PREFILL_REQUESTS, dtype=jnp.int32) == longest, CACHE_POSITIONS // REQUEST_TOKENS, step_count)
    return (step_count * REQUEST_TOKENS).astype(jnp.int32)


def states_draw(key, row_total):
    ramp = jnp.power(3.0, jnp.arange(D, dtype=jnp.float32) / D - 0.5)
    base_draw = normal_base(jax.random.fold_in(key, 1), (row_total, D))
    row_scale = jnp.exp(jax.random.uniform(jax.random.fold_in(key, 2), (row_total, 1), jnp.float32, -1.2, 1.2))
    return (base_draw * row_scale * ramp[None, :]).astype(jnp.bfloat16)


def draw_prefill_states(key, part):
    return states_draw(key, PREFILL_TOKENS)


def draw_decode_states(key, part):
    return states_draw(key, DECODE_REQUESTS)


def levels(rng, shape, shards, low, top_value):
    factor_of = 1.0
    for axis_at, blocks in shards:
        steps = jax.random.uniform(jax.random.fold_in(jax.random.fold_in(rng, 6), axis_at), (blocks,), jnp.float32, low / len(shards), top_value / len(shards))
        factor_of = factor_of * jnp.repeat(jnp.exp(steps), shape[axis_at] // blocks).reshape((-1,) + (1,) * (len(shape) - 1 - axis_at))
    return factor_of


def centred(own_key, shape, deviation, most, pieces=(), kind=jnp.bfloat16):
    values = jax.random.normal(own_key, shape, jnp.float32) * deviation
    if len(pieces) > 0:
        values = levels(own_key, shape, pieces, -0.22, 0.18) * values
    return jnp.clip(values, min=-most, max=most).astype(kind)


def setup_inputs(seed: int = 0) -> dict:
    keys = jax.random.split(jax.random.key(seed), 17)
    prefill_query = draw_prefill_query(jax.random.fold_in(keys[16], 71), 0)
    prefill_new_pairs = draw_prefill_new_pairs(jax.random.fold_in(keys[16], 71), 0)
    prefill_cache = draw_prefill_cache(jax.random.fold_in(keys[16], 71), 0)
    prefill_start = draw_prefill_start(jax.random.fold_in(keys[16], 71), 0)
    decode_query = draw_decode_query(jax.random.fold_in(keys[16], 71), 0)
    decode_fresh = draw_decode_fresh(jax.random.fold_in(keys[16], 71), 0)
    decode_cache = draw_decode_cache(jax.random.fold_in(keys[16], 71), 0)
    decode_length = draw_decode_length(jax.random.fold_in(keys[16], 71), 0)
    decode_slot = jax.random.permutation(keys[8], DECODE_REQUESTS).astype(jnp.int32)
    prefill_states = draw_prefill_states(jax.random.fold_in(keys[16], 71), 0)
    decode_states = draw_decode_states(jax.random.fold_in(keys[16], 71), 0)
    output_proj = centred(keys[11], (HQ * HEAD_SIZE, D), (HQ * HEAD_SIZE) ** -0.5, 0.125, ((0, 4), (1, 32)))
    norm_gain = jnp.clip(1.0 + 0.18 * jax.random.normal(keys[12], (D,), jnp.float32), 0.099609375, 1.8984375).astype(jnp.bfloat16)
    gate_weight = centred(keys[13], (D, FF), D ** -0.5, 0.125, ((0, 32), (1, 4)))
    up_weight = centred(keys[14], (D, FF), D ** -0.5, 0.125, ((0, 32), (1, 4)))
    down_weight = centred(keys[15], (FF, D), FF ** -0.5, 0.078125, ((0, 4), (1, 32)))
    return {"prefill_query": prefill_query, "prefill_new_pairs": prefill_new_pairs, "prefill_cache": prefill_cache, "prefill_start": prefill_start, "decode_query": decode_query, "decode_fresh": decode_fresh, "decode_cache": decode_cache, "decode_length": decode_length, "decode_slot": decode_slot, "prefill_states": prefill_states, "decode_states": decode_states, "output_proj": output_proj, "norm_gain": norm_gain, "gate_weight": gate_weight, "up_weight": up_weight, "down_weight": down_weight}


rope_base = 1000000.0
norm_eps = 1e-06

def rope_tables(positions, head_size):
    half_size = head_size // 2
    lane_index = jnp.arange(half_size, dtype=jnp.float32)
    inverse = jnp.power(jnp.float32(rope_base), -2.0 * lane_index / head_size)
    angles = positions.astype(jnp.float32)[:, None] * inverse[None, :]
    cosine = jnp.concatenate([jnp.cos(angles), jnp.cos(angles)], axis=1)
    sine_table = jnp.concatenate([jnp.sin(angles), jnp.sin(angles)], axis=1)
    return (cosine, sine_table)

def rotate(vectors, cosine, sine_table):
    half_size = vectors.shape[-1] // 2
    front_half = vectors[..., :half_size]
    back_half = vectors[..., half_size:]
    turned = jnp.concatenate([-back_half, front_half], axis=-1)
    return vectors * cosine[:, None, :] + turned * sine_table[:, None, :]

def attend(query_rows, key_rows, value_rows, visible):
    row_count, head_count, head_size = query_rows.shape
    groups = key_rows.shape[1]
    grouped = query_rows.reshape(row_count, groups, head_count // groups, head_size).astype(jnp.float32)
    scores = jnp.einsum('qhgd,khd->hgqk', grouped, key_rows.astype(jnp.float32)) * (1.0 / math.sqrt(head_size))
    scores = jnp.where(visible[None, None], scores, -jnp.inf)
    highest = lax.optimization_barrier(jnp.max(scores, axis=-1, keepdims=True))
    unnormed = jnp.exp(scores - highest)
    totals = lax.optimization_barrier(jnp.sum(unnormed, axis=-1, keepdims=True))
    rounded = unnormed.astype(jnp.bfloat16)
    blended = jnp.einsum('hgqk,khd->qhgd', rounded.astype(jnp.float32), value_rows.astype(jnp.float32))
    blended = blended / jnp.transpose(totals, (2, 0, 1, 3))
    return blended.reshape(row_count, head_count * head_size).astype(jnp.bfloat16)

def prefill_task(query_rows, fresh_rows, cache_rows, offset_value, head_size):
    span_len = query_rows.shape[0]
    positions = offset_value + jnp.arange(span_len, dtype=jnp.int32)
    cosine, sine_table = rope_tables(positions, head_size)
    head_count = query_rows.shape[1] // head_size
    groups = fresh_rows.shape[2] // head_size
    rot_query = rotate(query_rows.astype(jnp.float32).reshape(span_len, head_count, head_size), cosine, sine_table).astype(jnp.bfloat16)
    rot_key = rotate(fresh_rows[:, 0].astype(jnp.float32).reshape(span_len, groups, head_size), cosine, sine_table).astype(jnp.bfloat16)
    cache_len = cache_rows.shape[1]
    key_rows = jnp.concatenate([cache_rows[0].reshape(cache_len, groups, head_size), rot_key], axis=0)
    value_rows = jnp.concatenate([cache_rows[1].reshape(cache_len, groups, head_size), fresh_rows[:, 1].reshape(span_len, groups, head_size)], axis=0)
    cache_seen = jnp.broadcast_to(jnp.arange(cache_len, dtype=jnp.int32)[None, :] < offset_value, (span_len, cache_len))
    own_seen = jnp.arange(span_len, dtype=jnp.int32)[None, :] <= jnp.arange(span_len, dtype=jnp.int32)[:, None]
    visible = jnp.concatenate([cache_seen, own_seen], axis=1)
    return attend(rot_query, key_rows, value_rows, visible)

def decode_task(query_rows, fresh_rows, cache_rows, length, head_size):
    positions = jnp.reshape(length, (1,)).astype(jnp.int32)
    cosine, sine_table = rope_tables(positions, head_size)
    head_count = query_rows.shape[0] // head_size
    groups = fresh_rows.shape[1] // head_size
    rot_query = rotate(query_rows.astype(jnp.float32).reshape(1, head_count, head_size), cosine, sine_table).astype(jnp.bfloat16)
    rot_key = rotate(fresh_rows[0].astype(jnp.float32).reshape(1, groups, head_size), cosine, sine_table).astype(jnp.bfloat16)
    cache_len = cache_rows.shape[1]
    key_rows = jnp.concatenate([cache_rows[0].reshape(cache_len, groups, head_size), rot_key], axis=0)
    value_rows = jnp.concatenate([cache_rows[1].reshape(cache_len, groups, head_size), fresh_rows[1].reshape(1, groups, head_size)], axis=0)
    visible = jnp.concatenate([jnp.arange(cache_len, dtype=jnp.int32)[None, :] < length, jnp.ones((1, 1), jnp.bool_)], axis=1)
    return attend(rot_query, key_rows, value_rows, visible)[0]

def reference(prefill_query, prefill_new_pairs, prefill_cache, prefill_start, decode_query, decode_fresh, decode_cache, decode_length, decode_slot, prefill_states, decode_states, output_proj, norm_gain, gate_weight, up_weight, down_weight):
    query_blocks = prefill_query.reshape(PREFILL_REQUESTS, REQUEST_TOKENS, HQ * HEAD_SIZE)
    newest_blocks = prefill_new_pairs.reshape(PREFILL_REQUESTS, REQUEST_TOKENS, 2, KEY_VALUE_HEADS * HEAD_SIZE)
    prefill_att = lax.map(lambda operands: prefill_task(operands[0], operands[1], operands[2], operands[3], HEAD_SIZE), (query_blocks, newest_blocks, prefill_cache, prefill_start))
    prefill_att = prefill_att.reshape(PREFILL_TOKENS, HQ * HEAD_SIZE)
    slot_query = jnp.zeros_like(decode_query).at[decode_slot].set(decode_query)
    slot_fresh = jnp.zeros_like(decode_fresh).at[decode_slot].set(decode_fresh)
    slot_att = lax.map(lambda operands: decode_task(operands[0], operands[1], operands[2], operands[3], HEAD_SIZE), (slot_query, slot_fresh, decode_cache, decode_length))
    decode_att = slot_att[decode_slot]
    attended = jnp.concatenate([prefill_att, decode_att], axis=0)
    states = jnp.concatenate([prefill_states, decode_states], axis=0)
    summed = states.astype(jnp.float32) + jnp.dot(attended, output_proj, preferred_element_type=jnp.float32)
    mean_square = lax.optimization_barrier(jnp.mean(summed * summed, axis=1, keepdims=True))
    normed = (summed * lax.rsqrt(mean_square + norm_eps) * norm_gain.astype(jnp.float32)).astype(jnp.bfloat16)
    gate_sum = jnp.dot(normed, gate_weight, preferred_element_type=jnp.float32)
    upper = jnp.dot(normed, up_weight, preferred_element_type=jnp.float32)
    hidden = (jax.nn.silu(gate_sum) * upper).astype(jnp.bfloat16)
    result = (summed + jnp.dot(hidden, down_weight, preferred_element_type=jnp.float32)).astype(jnp.bfloat16)
    return (result[:PREFILL_TOKENS], result[PREFILL_TOKENS:])
```

```python
import math

import jax
import jax.numpy as jnp
from jax import lax
from jax.experimental import pallas as pl
from jax.experimental.pallas import tpu as pltpu
from jax.sharding import Mesh
from jax.sharding import PartitionSpec as P


F32 = jnp.float32
BF16 = jnp.bfloat16
HEAD_SIZE = 128
NEW = 512
ROWS = 528
EXTRA = 16
SPLIT = 256
BLOCK = 512
WIDTH = 2048
CACHE = 2048
HIDDEN = 1536
rope_base = 1000000.0
norm_eps = 1e-06
EXP_SCALE = math.log2(math.e) / math.sqrt(HEAD_SIZE)
UNSEEN = -1e30
NT = (((1,), (1,)), ((), ()))
TN = (((0,), (0,)), ((), ()))
VMEM_LIMIT = 58 * 1024 * 1024

START, LENGTH, SLOT, AT_X, AT_Y, AT_CORE, AT_HEAD, OWNER = 0, 1, 4, 7, 8, 9, 10, 11


def mm(a, b, dims=(((1,), (0,)), ((), ()))):
    return lax.dot_general(a, b, dims, preferred_element_type=F32)


def rope_tables(positions, head_size):
    half_size = head_size // 2
    lane_index = jnp.arange(half_size, dtype=F32)
    inverse = jnp.power(F32(rope_base), -2.0 * lane_index / head_size)
    angles = positions.astype(F32)[:, None] * inverse[None, :]
    cosine, sine = jnp.cos(angles), jnp.sin(angles)
    return (
        jnp.concatenate([cosine, cosine], axis=1),
        jnp.concatenate([-sine, sine], axis=1),
    )


def turn(values, cosine, signed_sine):
    return values * cosine + pltpu.roll(values, HEAD_SIZE // 2, 1) * signed_sine


def prefill_kernel(info, q_ref, kf_ref, vf_ref, c_ref, cos_ref, sin_ref, o_ref, kr, qr):
    cosine, sine = cos_ref[...], sin_ref[...]
    kr[...] = turn(kf_ref[...].astype(F32), cosine, sine).astype(BF16)
    for h in range(2):
        lanes = slice(h * HEAD_SIZE, (h + 1) * HEAD_SIZE)
        qr[:, lanes] = turn(q_ref[:, lanes].astype(F32), cosine, sine).astype(BF16)
    start = info[START]

    def run(length, masked):
        old_keys = c_ref[0, 0, :length, :]
        old_values = c_ref[0, 1, :length, :]
        for r in range(NEW // SPLIT):
            seen = (r + 1) * SPLIT
            for h in range(2):
                q = qr[r * SPLIT : seen, h * HEAD_SIZE : (h + 1) * HEAD_SIZE]
                old = mm(q, old_keys, NT)
                if masked:
                    at = lax.broadcasted_iota(jnp.int32, old.shape, 1)
                    old = jnp.where(at < start, old, UNSEEN)
                new = mm(q, kr[:seen, :], NT)
                row = lax.broadcasted_iota(jnp.int32, new.shape, 0) + r * SPLIT
                col = lax.broadcasted_iota(jnp.int32, new.shape, 1)
                new = jnp.where(col <= row, new, UNSEEN)
                top = jnp.maximum(
                    jnp.max(old, axis=1, keepdims=True), jnp.max(new, axis=1, keepdims=True)
                )
                old = jnp.exp2((old - top) * EXP_SCALE)
                new = jnp.exp2((new - top) * EXP_SCALE)
                total = jnp.sum(old, axis=1, keepdims=True) + jnp.sum(new, axis=1, keepdims=True)
                blend = mm(old.astype(BF16), old_values) + mm(new.astype(BF16), vf_ref[:seen, :])
                o_ref[r * SPLIT : seen, h * HEAD_SIZE : (h + 1) * HEAD_SIZE] = (
                    blend / total
                ).astype(BF16)

    @pl.when(start >= CACHE)
    def _():
        run(CACHE, False)

    @pl.when(start < CACHE)
    def _():
        run(CACHE - NEW, True)


def prefill_group(group, info, query, fresh, cache, cosine, sine):
    grid = pltpu.PrefetchScalarGridSpec(
        num_scalar_prefetch=1,
        grid=(1,),
        in_specs=[
            pl.BlockSpec((NEW, 2 * HEAD_SIZE), lambda i, s: (0, group)),
            pl.BlockSpec((NEW, HEAD_SIZE), lambda i, s: (0, group)),
            pl.BlockSpec((NEW, HEAD_SIZE), lambda i, s: (0, 2 + group)),
            pl.BlockSpec((1, 2, CACHE, HEAD_SIZE), lambda i, s: (0, 0, 0, group)),
            pl.BlockSpec((NEW, HEAD_SIZE), lambda i, s: (0, 0)),
            pl.BlockSpec((NEW, HEAD_SIZE), lambda i, s: (0, 0)),
        ],
        out_specs=pl.BlockSpec((NEW, 2 * HEAD_SIZE), lambda i, s: (0, 0)),
        scratch_shapes=[
            pltpu.VMEM((NEW, HEAD_SIZE), BF16),
            pltpu.VMEM((NEW, 2 * HEAD_SIZE), BF16),
        ],
    )
    return pl.pallas_call(
        prefill_kernel,
        grid_spec=grid,
        out_shape=jax.ShapeDtypeStruct((NEW, 2 * HEAD_SIZE), BF16),
        compiler_params=pltpu.CompilerParams(vmem_limit_bytes=VMEM_LIMIT),
        cost_estimate=pl.CostEstimate(
            flops=4 * NEW * 2 * HEAD_SIZE * (CACHE + NEW),
            transcendentals=NEW * 2 * (CACHE + NEW),
            bytes_accessed=3 * 1024 * 1024,
        ),
        name=f"prefill_group_{group}",
    )(info, query, fresh, fresh, cache, cosine, sine)


def decode_kernel(info, tok_ref, c_ref, cos_ref, sin_ref, o_ref, q_sc, f_sc, o_sc):
    s = pl.program_id(0)

    @pl.when(s == 0)
    def _():
        code = tok_ref[:, BLOCK : BLOCK + 8].astype(F32)
        want = info[OWNER] * 3 + lax.broadcasted_iota(jnp.int32, code.shape, 1)
        lane = lax.broadcasted_iota(jnp.int32, code.shape, 1)
        want = jnp.where(lane < 3, want, 1000).astype(F32)
        packed = tok_ref[:, :BLOCK]
        q = mm((code == want).astype(F32).astype(BF16), packed, TN)
        f = mm((code == want + 96.0).astype(F32).astype(BF16), packed, TN)
        cosine, sine = cos_ref[...], sin_ref[...]
        for h in range(4):
            lanes = slice(h * HEAD_SIZE, (h + 1) * HEAD_SIZE)
            q_sc[:, lanes] = turn(q[:, lanes], cosine, sine).astype(BF16).astype(F32)
            if h < 2:
                f_sc[:, lanes] = turn(f[:, lanes], cosine, sine).astype(BF16).astype(F32)
            else:
                f_sc[:, lanes] = f[:, lanes]
        o_sc[...] = jnp.zeros_like(o_sc)

    length = info[LENGTH + s]
    mine = lax.broadcasted_iota(jnp.int32, (8, BLOCK), 0) == s
    q = jnp.sum(jnp.where(mine, q_sc[...], 0.0), axis=0, keepdims=True)
    f = jnp.sum(jnp.where(mine, f_sc[...], 0.0), axis=0, keepdims=True)
    row = lax.broadcasted_iota(jnp.int32, (8, HEAD_SIZE), 0)

    def place(a, b):
        left = jnp.broadcast_to(q[:, a * HEAD_SIZE : (a + 1) * HEAD_SIZE], (8, HEAD_SIZE))
        right = jnp.broadcast_to(q[:, b * HEAD_SIZE : (b + 1) * HEAD_SIZE], (8, HEAD_SIZE))
        return jnp.where(row == a, left, jnp.where(row == b, right, 0.0))

    wide = jnp.concatenate([place(0, 1), place(2, 3)], axis=1)
    scores = mm(wide.astype(BF16), c_ref[0, 0], NT)
    at = lax.broadcasted_iota(jnp.int32, scores.shape, 1)
    scores = jnp.where(at < length, scores, UNSEEN)
    own = jnp.sum(wide * f[:, : 2 * HEAD_SIZE], axis=1, keepdims=True)
    top = jnp.maximum(jnp.max(scores, axis=1, keepdims=True), own)
    raw = jnp.exp2((scores - top) * EXP_SCALE)
    raw_own = jnp.exp2((own - top) * EXP_SCALE)
    total = jnp.sum(raw, axis=1, keepdims=True) + raw_own
    blend = mm(raw.astype(BF16), c_ref[0, 1])
    blend = blend + raw_own.astype(BF16).astype(F32) * f[:, 2 * HEAD_SIZE :]
    blend = blend / total
    upper = jnp.concatenate([blend[0:1, :HEAD_SIZE], blend[1:2, :HEAD_SIZE]], axis=1)
    lower = jnp.concatenate([blend[2:3, HEAD_SIZE:], blend[3:4, HEAD_SIZE:]], axis=1)
    row = lax.broadcasted_iota(jnp.int32, (8, 2 * HEAD_SIZE), 0)
    o_sc[...] = jnp.where(row == s, upper, jnp.where(row == s + 3, lower, o_sc[...]))

    @pl.when(s == 2)
    def _():
        o_ref[...] = o_sc[...].astype(BF16)


def decode_call(info, tokens, cache, cosine, sine):
    grid = pltpu.PrefetchScalarGridSpec(
        num_scalar_prefetch=1,
        grid=(3,),
        in_specs=[
            pl.BlockSpec((256, 640), lambda i, s: (0, 0)),
            pl.BlockSpec((1, 2, CACHE, 2 * HEAD_SIZE), lambda i, s: (i, 0, 0, 0)),
            pl.BlockSpec((8, HEAD_SIZE), lambda i, s: (NEW // 8, 0)),
            pl.BlockSpec((8, HEAD_SIZE), lambda i, s: (NEW // 8, 0)),
        ],
        out_specs=pl.BlockSpec((8, 2 * HEAD_SIZE), lambda i, s: (0, 0)),
        scratch_shapes=[
            pltpu.VMEM((8, 4 * HEAD_SIZE), F32),
            pltpu.VMEM((8, 4 * HEAD_SIZE), F32),
            pltpu.VMEM((8, 2 * HEAD_SIZE), F32),
        ],
    )
    return pl.pallas_call(
        decode_kernel,
        grid_spec=grid,
        out_shape=jax.ShapeDtypeStruct((8, 2 * HEAD_SIZE), BF16),
        compiler_params=pltpu.CompilerParams(vmem_limit_bytes=VMEM_LIMIT),
        cost_estimate=pl.CostEstimate(
            flops=3 * 4 * 256 * CACHE * 256, transcendentals=0, bytes_accessed=7 * 1024 * 1024
        ),
        name="decode_attention",
    )(info, tokens, cache, cosine, sine)


def project_kernel(
    info, a0_ref, a1_ref, dec_ref, w0_ref, w1_ref, ps_ref, ds_ref, own_ref, o1, o2, o3, a_sc, w_sc
):
    x, y, core, head, owner = (info[i] for i in (AT_X, AT_Y, AT_CORE, AT_HEAD, OWNER))
    a_sc[:NEW, : 2 * HEAD_SIZE] = a0_ref[...]
    a_sc[:NEW, 2 * HEAD_SIZE :] = a1_ref[...]
    shape = (256, EXTRA)
    row = lax.broadcasted_iota(jnp.int32, shape, 0)
    lane = lax.broadcasted_iota(jnp.int32, shape, 1)
    mine = jnp.full(shape, -1, jnp.int32)
    for t in range(3):
        mine = jnp.where(lane == t, info[SLOT + t], mine)
    piece, place = row >> 3, row & 7
    mask = jnp.zeros_like(piece)
    for b in range(5):
        mask = mask | (((piece >> b) & 1) << (4 - b))
    first = (mask ^ owner) * 3
    for g in range(2):
        at = place - 3 * g
        pick = (at >= 0) & (at < 3) & (first + at == mine)
        chosen = mm(pick.astype(F32).astype(BF16), dec_ref[...], TN)
        a_sc[NEW:, g * 2 * HEAD_SIZE : (g + 1) * 2 * HEAD_SIZE] = chosen.astype(BF16)
    for xi in range(4):
        for yi in range(4):
            place_in = (lax.bitwise_xor(x, xi) * 4 + lax.bitwise_xor(y, yi)) * 64
            place_in = pl.multiple_of(place_in, 64)
            to = (xi * 8 + yi * 2) * 64

            @pl.when(core == 0)
            def _():
                w_sc[to : to + 64, :] = w0_ref[pl.ds(place_in, 64), :]
                w_sc[to + 64 : to + 128, :] = w1_ref[pl.ds(place_in, 64), :]

            @pl.when(core == 1)
            def _():
                w_sc[to : to + 64, :] = w1_ref[pl.ds(place_in, 64), :]
                w_sc[to + 64 : to + 128, :] = w0_ref[pl.ds(place_in, 64), :]

    for k, out in enumerate((own_ref, o1, o2, o3)):
        at = pl.multiple_of(lax.bitwise_xor(head, k) * BLOCK, BLOCK)
        part = mm(a_sc[...], w_sc[pl.ds(at, BLOCK), :], NT)
        if k == 0:
            out[:NEW, :] = part[:NEW, :] + ps_ref[...].astype(F32)
            out[NEW:, :] = part[NEW:, :]
            out[NEW : NEW + 3, :] = part[NEW : NEW + 3, :] + ds_ref[...].astype(F32)
        else:
            out[...] = part.astype(BF16)


VM = pl.BlockSpec(memory_space=pltpu.VMEM)
SM = pl.BlockSpec(memory_space=pltpu.SMEM)


def project_call(info, a0, a1, dec, w0, w1, prefill_states, decode_states):
    return pl.pallas_call(
        project_kernel,
        in_specs=[SM] + [VM] * 7,
        out_specs=[VM] * 4,
        out_shape=[jax.ShapeDtypeStruct((ROWS, BLOCK), F32)]
        + [jax.ShapeDtypeStruct((ROWS, BLOCK), BF16)] * 3,
        scratch_shapes=[pltpu.VMEM((ROWS, BLOCK), BF16), pltpu.VMEM((WIDTH, BLOCK), BF16)],
        compiler_params=pltpu.CompilerParams(vmem_limit_bytes=VMEM_LIMIT),
        cost_estimate=pl.CostEstimate(
            flops=2 * ROWS * BLOCK * WIDTH, transcendentals=0, bytes_accessed=6 * 1024 * 1024
        ),
        name="project",
    )(info, a0, a1, dec, w0, w1, prefill_states, decode_states)


def combine_kernel(info, gain_ref, own_ref, r1, r2, r3, summed_ref, g_ref):
    total = own_ref[...] + r1[...].astype(F32) + r2[...].astype(F32) + r3[...].astype(F32)
    summed_ref[...] = total
    at = pl.multiple_of(info[AT_HEAD] * BLOCK, BLOCK)
    g_ref[...] = (total * gain_ref[:, pl.ds(at, BLOCK)].astype(F32)).astype(BF16)


def combine_call(info, gain, own, parts):
    return pl.pallas_call(
        combine_kernel,
        in_specs=[SM] + [VM] * 5,
        out_specs=[VM] * 2,
        out_shape=[
            jax.ShapeDtypeStruct((ROWS, BLOCK), F32),
            jax.ShapeDtypeStruct((ROWS, BLOCK), BF16),
        ],
        compiler_params=pltpu.CompilerParams(vmem_limit_bytes=VMEM_LIMIT),
        name="combine",
    )(info, gain, own, *parts)


STEP = 256
GATE_STEPS = HIDDEN // STEP


def ffn_kernel(
    low, high, info, g0, g1, g2, g3, gain_ref, wg, wu, wd, own_ref, o1, o2, o3, n_sc, r_sc, h_sc
):
    i = pl.program_id(0)
    head = info[AT_HEAD]

    @pl.when(i == 0)
    def _():
        squares = jnp.zeros((high - low, 1), F32)
        for k, part in enumerate((g0, g1, g2, g3)):
            at = pl.multiple_of(lax.bitwise_xor(head, k) * BLOCK, BLOCK)
            value = part[low:high, :]
            n_sc[:, pl.ds(at, BLOCK)] = value
            plain = value.astype(F32) / gain_ref[:, pl.ds(at, BLOCK)].astype(F32)
            squares = squares + jnp.sum(plain * plain, axis=1, keepdims=True)
        r_sc[...] = jnp.broadcast_to(lax.rsqrt(squares * (1.0 / WIDTH) + norm_eps), r_sc.shape)

    @pl.when(i < GATE_STEPS)
    def _():
        scale = r_sc[:, :1]
        gate = mm(n_sc[...], wg[...]) * scale
        upper = mm(n_sc[...], wu[...]) * scale
        hidden = gate / (1.0 + jnp.exp(-gate)) * upper
        at = pl.multiple_of(i * STEP, STEP)
        h_sc[:, pl.ds(at, STEP)] = hidden.astype(BF16)

    for k, out in enumerate((own_ref, o1, o2, o3)):

        @pl.when(i == GATE_STEPS + k)
        def _():
            out[...] = mm(h_sc[...], wd[...], NT).astype(out.dtype)


def ffn_call(low, high, info, parts, gain, weights):
    rows = high - low
    last = GATE_STEPS - 1

    def down_map(i, s):
        return (lax.bitwise_xor(s[AT_HEAD], jnp.maximum(i - GATE_STEPS, 0)), 2)

    whole = pl.BlockSpec((ROWS, BLOCK), lambda i, s: (0, 0))
    out = pl.BlockSpec((rows, BLOCK), lambda i, s: (0, 0))
    grid = pltpu.PrefetchScalarGridSpec(
        num_scalar_prefetch=1,
        grid=(GATE_STEPS + 4,),
        in_specs=[whole] * 4
        + [
            pl.BlockSpec((1, WIDTH), lambda i, s: (0, 0)),
            pl.BlockSpec((WIDTH, STEP), lambda i, s: (0, jnp.minimum(i, last))),
            pl.BlockSpec((WIDTH, STEP), lambda i, s: (0, GATE_STEPS + jnp.minimum(i, last))),
            pl.BlockSpec((BLOCK, HIDDEN), down_map),
        ],
        out_specs=[out] * 4,
        scratch_shapes=[
            pltpu.VMEM((rows, WIDTH), BF16),
            pltpu.VMEM((rows, 128), F32),
            pltpu.VMEM((rows, HIDDEN), BF16),
        ],
    )

    def kernel(*refs):
        ffn_kernel(low, high, *refs)

    return pl.pallas_call(
        kernel,
        grid_spec=grid,
        out_shape=[jax.ShapeDtypeStruct((rows, BLOCK), F32)]
        + [jax.ShapeDtypeStruct((rows, BLOCK), BF16)] * 3,
        compiler_params=pltpu.CompilerParams(vmem_limit_bytes=VMEM_LIMIT),
        cost_estimate=pl.CostEstimate(
            flops=6 * rows * HIDDEN * WIDTH,
            transcendentals=rows * HIDDEN,
            bytes_accessed=20 * 1024 * 1024,
        ),
        name=f"ffn_{low}",
    )(info, *parts, gain, weights, weights, weights)


def finish_kernel(s_ref, oa, a1, a2, a3, ob, b1, b2, b3, p_ref, d_ref):
    def added(low, high, own, r1, r2, r3):
        total = s_ref[low:high, :] + own[...]
        return total + r1[...].astype(F32) + r2[...].astype(F32) + r3[...].astype(F32)

    p_ref[:SPLIT, :] = added(0, SPLIT, oa, a1, a2, a3).astype(BF16)
    rest = added(SPLIT, ROWS, ob, b1, b2, b3).astype(BF16)
    p_ref[SPLIT:, :] = rest[: NEW - SPLIT, :]
    d_ref[...] = rest[NEW - SPLIT : NEW - SPLIT + 3, :]


def finish_call(summed, first, second):
    return pl.pallas_call(
        finish_kernel,
        in_specs=[VM] * 9,
        out_specs=[VM] * 2,
        out_shape=[
            jax.ShapeDtypeStruct((NEW, BLOCK), BF16),
            jax.ShapeDtypeStruct((3, BLOCK), BF16),
        ],
        compiler_params=pltpu.CompilerParams(vmem_limit_bytes=VMEM_LIMIT),
        name="finish",
    )(summed, *first, *second)


SIZE = {"x": 4, "y": 4, "core": 2, "head": 4}


def swap(value, axis, k):
    return lax.ppermute(value, axis, [(i, i ^ k) for i in range(SIZE[axis])])


def doubled(value):
    for axis, k in (("x", 2), ("x", 1), ("y", 2), ("y", 1), ("core", 1)):
        value = jnp.concatenate([value, swap(value, axis, k)], axis=0)
    return value


def body(
    prefill_query,
    prefill_new_pairs,
    prefill_cache,
    prefill_start,
    decode_query,
    decode_fresh,
    decode_cache,
    decode_length,
    decode_slot,
    prefill_states,
    decode_states,
    output_proj,
    norm_gain,
    gate_weight,
    up_weight,
    down_weight,
):
    at = [lax.axis_index(a) for a in ("x", "y", "core", "head")]
    owner = at[0] * 8 + at[1] * 2 + at[2]
    info = jnp.concatenate(
        [prefill_start, decode_length, decode_slot, jnp.stack(at + [owner]).astype(jnp.int32)]
    )

    packed = jnp.concatenate([gate_weight, up_weight, down_weight.T], axis=1)
    weights = lax.all_gather(packed, ("x", "y", "core"), axis=0, tiled=True)

    code = decode_slot.astype(BF16)[:, None]
    lanes = jnp.ones((1, 128), BF16)
    tokens = jnp.concatenate(
        [
            jnp.concatenate([decode_query, code * lanes], axis=1),
            jnp.concatenate([decode_fresh.reshape(3, BLOCK), (code + 96.0).astype(BF16) * lanes], axis=1),
            jnp.full((2, BLOCK + 128), 255.0, BF16),
        ],
        axis=0,
    )
    tokens = doubled(tokens)

    piece = output_proj.T
    for axis in ("y", "x"):
        piece = jnp.concatenate([piece] + [swap(piece, axis, k) for k in (1, 2, 3)], axis=0)
    other = swap(piece, "core", 1)

    positions = jnp.concatenate(
        [
            prefill_start + jnp.arange(NEW, dtype=jnp.int32),
            decode_length,
            jnp.zeros((5,), jnp.int32),
        ]
    )
    cosine, sine = rope_tables(positions, HEAD_SIZE)
    fresh = prefill_new_pairs.reshape(NEW, BLOCK)
    decoded = decode_call(info, tokens, decode_cache, cosine, sine)
    decoded = doubled(decoded)
    att = [
        prefill_group(g, info, prefill_query, fresh, prefill_cache, cosine, sine) for g in range(2)
    ]
    own, *parts = project_call(
        info, att[0], att[1], decoded, piece, other, prefill_states, decode_states
    )
    gain = norm_gain.reshape(1, WIDTH)
    summed, scaled = combine_call(
        info, gain, own, [swap(p, "head", k + 1) for k, p in enumerate(parts)]
    )
    whole = [scaled] + [swap(scaled, "head", k) for k in (1, 2, 3)]
    halves = []
    for low, high in ((0, SPLIT), (SPLIT, ROWS)):
        own, *parts = ffn_call(low, high, info, whole, gain, weights)
        halves.append([own] + [swap(p, "head", k + 1) for k, p in enumerate(parts)])
    return finish_call(summed, halves[0], halves[1])


def solution(mesh):
    inner = Mesh(mesh.devices.reshape(4, 4, 2, 4), ("x", "y", "core", "head"))
    req = ("x", "y", "core")
    in_specs = (
        P(req, "head"),
        P(req, None, "head"),
        P(req, None, None, "head"),
        P(req),
        P(req, "head"),
        P(req, None, "head"),
        P(req, None, None, "head"),
        P(req),
        P(req),
        P(req, "head"),
        P(req, "head"),
        P("head", req),
        P(),
        P(req, "head"),
        P(req, "head"),
        P("head", req),
    )
    out_specs = (P(req, "head"), P(req, "head"))
    return jax.shard_map(body, mesh=inner, in_specs=in_specs, out_specs=out_specs, check_vma=False)
```

```python
import math

import jax
import jax.numpy as jnp
from jax import lax
from jax.experimental import pallas as pl
from jax.experimental.pallas import tpu as pltpu
from jax.sharding import Mesh
from jax.sharding import PartitionSpec as P


F32 = jnp.float32
BF16 = jnp.bfloat16
HEAD_SIZE = 128
NEW = 512
EXTRA = 16
SPLIT = 256
BLOCK = 512
WIDTH = 2048
CACHE = 2048
HIDDEN = 1536
PIECE = 80
rope_base = 1000000.0
norm_eps = 1e-06
EXP_SCALE = math.log2(math.e) / math.sqrt(HEAD_SIZE)
UNSEEN = -1e30
NT = (((1,), (1,)), ((), ()))
TN = (((0,), (0,)), ((), ()))
VMEM_LIMIT = 58 * 1024 * 1024

START, LENGTH, SLOT, AT_X, AT_Y, AT_CORE, AT_HEAD, OWNER = 0, 1, 4, 7, 8, 9, 10, 11


def mm(a, b, dims=(((1,), (0,)), ((), ()))):
    return lax.dot_general(a, b, dims, preferred_element_type=F32)


def rope_tables(positions, head_size):
    half_size = head_size // 2
    lane_index = jnp.arange(half_size, dtype=F32)
    inverse = jnp.power(F32(rope_base), -2.0 * lane_index / head_size)
    angles = positions.astype(F32)[:, None] * inverse[None, :]
    cosine, sine = jnp.cos(angles), jnp.sin(angles)
    return (
        jnp.concatenate([cosine, cosine], axis=1),
        jnp.concatenate([-sine, sine], axis=1),
    )


def turn(values, cosine, signed_sine):
    return values * cosine + pltpu.roll(values, HEAD_SIZE // 2, 1) * signed_sine


def prefill_kernel(info, q_ref, kf_ref, vf_ref, c_ref, cos_ref, sin_ref, o_ref, kr, qr):
    cosine, sine = cos_ref[...], sin_ref[...]
    kr[...] = turn(kf_ref[...].astype(F32), cosine, sine).astype(BF16)
    for h in range(2):
        lanes = slice(h * HEAD_SIZE, (h + 1) * HEAD_SIZE)
        qr[:, lanes] = turn(q_ref[:, lanes].astype(F32), cosine, sine).astype(BF16)
    start = info[START]

    def run(length, masked):
        old_keys = c_ref[0, 0, :length, :]
        old_values = c_ref[0, 1, :length, :]
        for r in range(NEW // SPLIT):
            seen = (r + 1) * SPLIT
            for h in range(2):
                q = qr[r * SPLIT : seen, h * HEAD_SIZE : (h + 1) * HEAD_SIZE]
                old = mm(q, old_keys, NT)
                if masked:
                    at = lax.broadcasted_iota(jnp.int32, old.shape, 1)
                    old = jnp.where(at < start, old, UNSEEN)
                new = mm(q, kr[:seen, :], NT)
                row = lax.broadcasted_iota(jnp.int32, new.shape, 0) + r * SPLIT
                col = lax.broadcasted_iota(jnp.int32, new.shape, 1)
                new = jnp.where(col <= row, new, UNSEEN)
                top = jnp.maximum(
                    jnp.max(old, axis=1, keepdims=True), jnp.max(new, axis=1, keepdims=True)
                )
                old = jnp.exp2((old - top) * EXP_SCALE)
                new = jnp.exp2((new - top) * EXP_SCALE)
                total = jnp.sum(old, axis=1, keepdims=True) + jnp.sum(new, axis=1, keepdims=True)
                blend = mm(old.astype(BF16), old_values) + mm(new.astype(BF16), vf_ref[:seen, :])
                o_ref[r * SPLIT : seen, h * HEAD_SIZE : (h + 1) * HEAD_SIZE] = (
                    blend / total
                ).astype(BF16)

    @pl.when(start >= CACHE)
    def _():
        run(CACHE, False)

    @pl.when(start < CACHE)
    def _():
        run(CACHE - NEW, True)


def prefill_call(info, query, fresh, cache, cosine, sine):
    grid = pltpu.PrefetchScalarGridSpec(
        num_scalar_prefetch=1,
        grid=(2,),
        in_specs=[
            pl.BlockSpec((NEW, 2 * HEAD_SIZE), lambda i, s: (0, i)),
            pl.BlockSpec((NEW, HEAD_SIZE), lambda i, s: (0, i)),
            pl.BlockSpec((NEW, HEAD_SIZE), lambda i, s: (0, 2 + i)),
            pl.BlockSpec((1, 2, CACHE, HEAD_SIZE), lambda i, s: (0, 0, 0, i)),
            pl.BlockSpec((NEW, HEAD_SIZE), lambda i, s: (0, 0)),
            pl.BlockSpec((NEW, HEAD_SIZE), lambda i, s: (0, 0)),
        ],
        out_specs=pl.BlockSpec((NEW, 2 * HEAD_SIZE), lambda i, s: (0, i)),
        scratch_shapes=[
            pltpu.VMEM((NEW, HEAD_SIZE), BF16),
            pltpu.VMEM((NEW, 2 * HEAD_SIZE), BF16),
        ],
    )
    return pl.pallas_call(
        prefill_kernel,
        grid_spec=grid,
        out_shape=jax.ShapeDtypeStruct((NEW, 4 * HEAD_SIZE), BF16),
        compiler_params=pltpu.CompilerParams(vmem_limit_bytes=VMEM_LIMIT),
        cost_estimate=pl.CostEstimate(
            flops=4 * NEW * 4 * HEAD_SIZE * (CACHE + NEW),
            transcendentals=NEW * 4 * (CACHE + NEW),
            bytes_accessed=4 * 1024 * 1024,
        ),
        name="prefill_attention",
    )(info, query, fresh, fresh, cache, cosine, sine)


def decode_kernel(info, t0_ref, t1_ref, c_ref, cos_ref, sin_ref, o_ref, q_sc, f_sc, o_sc):
    s = pl.program_id(0)

    @pl.when(s == 0)
    def _():
        both = [r[...] for r in (t0_ref, t1_ref)]
        packed = jnp.concatenate([v[:, :8, :].reshape(128, BLOCK) for v in both], axis=0)
        code = jnp.concatenate([v[:, 8:, :128].reshape(128, 128) for v in both], axis=0)
        code = code[:, :8].astype(F32)
        want = info[OWNER] * 3 + lax.broadcasted_iota(jnp.int32, code.shape, 1)
        lane = lax.broadcasted_iota(jnp.int32, code.shape, 1)
        want = jnp.where(lane < 3, want, 1000).astype(F32)
        q = mm((code == want).astype(F32).astype(BF16), packed, TN)
        f = mm((code == want + 96.0).astype(F32).astype(BF16), packed, TN)
        cosine, sine = cos_ref[...], sin_ref[...]
        for h in range(4):
            lanes = slice(h * HEAD_SIZE, (h + 1) * HEAD_SIZE)
            q_sc[:, lanes] = turn(q[:, lanes], cosine, sine).astype(BF16).astype(F32)
            if h < 2:
                f_sc[:, lanes] = turn(f[:, lanes], cosine, sine).astype(BF16).astype(F32)
            else:
                f_sc[:, lanes] = f[:, lanes]
        o_sc[...] = jnp.zeros_like(o_sc)

    length = info[LENGTH + s]
    mine = lax.broadcasted_iota(jnp.int32, (8, BLOCK), 0) == s
    q = jnp.sum(jnp.where(mine, q_sc[...], 0.0), axis=0, keepdims=True)
    f = jnp.sum(jnp.where(mine, f_sc[...], 0.0), axis=0, keepdims=True)
    row = lax.broadcasted_iota(jnp.int32, (8, HEAD_SIZE), 0)

    def place(a, b):
        left = jnp.broadcast_to(q[:, a * HEAD_SIZE : (a + 1) * HEAD_SIZE], (8, HEAD_SIZE))
        right = jnp.broadcast_to(q[:, b * HEAD_SIZE : (b + 1) * HEAD_SIZE], (8, HEAD_SIZE))
        return jnp.where(row == a, left, jnp.where(row == b, right, 0.0))

    wide = jnp.concatenate([place(0, 1), place(2, 3)], axis=1)
    scores = mm(wide.astype(BF16), c_ref[0, 0], NT)
    at = lax.broadcasted_iota(jnp.int32, scores.shape, 1)
    scores = jnp.where(at < length, scores, UNSEEN)
    own = jnp.sum(wide * f[:, : 2 * HEAD_SIZE], axis=1, keepdims=True)
    top = jnp.maximum(jnp.max(scores, axis=1, keepdims=True), own)
    raw = jnp.exp2((scores - top) * EXP_SCALE)
    raw_own = jnp.exp2((own - top) * EXP_SCALE)
    total = jnp.sum(raw, axis=1, keepdims=True) + raw_own
    blend = mm(raw.astype(BF16), c_ref[0, 1])
    blend = blend + raw_own.astype(BF16).astype(F32) * f[:, 2 * HEAD_SIZE :]
    blend = blend / total
    upper = jnp.concatenate([blend[0:1, :HEAD_SIZE], blend[1:2, :HEAD_SIZE]], axis=1)
    lower = jnp.concatenate([blend[2:3, HEAD_SIZE:], blend[3:4, HEAD_SIZE:]], axis=1)
    row = lax.broadcasted_iota(jnp.int32, (8, 2 * HEAD_SIZE), 0)
    o_sc[...] = jnp.where(row == s, upper, jnp.where(row == s + 3, lower, o_sc[...]))

    @pl.when(s == 2)
    def _():
        o_ref[...] = o_sc[...].astype(BF16)


def decode_call(info, piece, other, cache, cosine, sine):
    grid = pltpu.PrefetchScalarGridSpec(
        num_scalar_prefetch=1,
        grid=(3,),
        in_specs=[
            pl.BlockSpec((16, 16, BLOCK), lambda i, s: (0, 4, 0)),
            pl.BlockSpec((16, 16, BLOCK), lambda i, s: (0, 4, 0)),
            pl.BlockSpec((1, 2, CACHE, 2 * HEAD_SIZE), lambda i, s: (i, 0, 0, 0)),
            pl.BlockSpec((8, HEAD_SIZE), lambda i, s: (NEW // 8, 0)),
            pl.BlockSpec((8, HEAD_SIZE), lambda i, s: (NEW // 8, 0)),
        ],
        out_specs=pl.BlockSpec((8, 2 * HEAD_SIZE), lambda i, s: (0, 0)),
        scratch_shapes=[
            pltpu.VMEM((8, 4 * HEAD_SIZE), F32),
            pltpu.VMEM((8, 4 * HEAD_SIZE), F32),
            pltpu.VMEM((8, 2 * HEAD_SIZE), F32),
        ],
    )
    return pl.pallas_call(
        decode_kernel,
        grid_spec=grid,
        out_shape=jax.ShapeDtypeStruct((8, 2 * HEAD_SIZE), BF16),
        compiler_params=pltpu.CompilerParams(vmem_limit_bytes=VMEM_LIMIT),
        cost_estimate=pl.CostEstimate(
            flops=3 * 4 * 256 * CACHE * 256, transcendentals=0, bytes_accessed=7 * 1024 * 1024
        ),
        name="decode_attention",
    )(info, piece, other, cache, cosine, sine)


def project_rows(info, a_ref, w_ref, ps_ref, outs):
    for k, out in enumerate(outs):
        at = pl.multiple_of(lax.bitwise_xor(info[AT_HEAD], k) * BLOCK, BLOCK)
        part = mm(a_ref[...], w_ref[pl.ds(at, BLOCK), :], NT)
        if k == 0:
            out[...] = part + ps_ref[...].astype(F32)
        else:
            out[...] = part.astype(BF16)


def project_first(info, a_ref, ps_ref, w0_ref, w1_ref, own, o1, o2, o3, w_out):
    x, y, core = (info[i] for i in (AT_X, AT_Y, AT_CORE))
    for xi in range(4):
        for yi in range(4):
            place = (lax.bitwise_xor(x, xi) * 4 + lax.bitwise_xor(y, yi)) * PIECE
            place = pl.multiple_of(place, 16)
            to = (xi * 8 + yi * 2) * 64

            @pl.when(core == 0)
            def _():
                w_out[to : to + 64, :] = w0_ref[pl.ds(place, 64), :]
                w_out[to + 64 : to + 128, :] = w1_ref[pl.ds(place, 64), :]

            @pl.when(core == 1)
            def _():
                w_out[to : to + 64, :] = w1_ref[pl.ds(place, 64), :]
                w_out[to + 64 : to + 128, :] = w0_ref[pl.ds(place, 64), :]

    project_rows(info, a_ref, w_out, ps_ref, (own, o1, o2, o3))


def project_second(info, a_ref, ps_ref, w_ref, own, o1, o2, o3):
    project_rows(info, a_ref, w_ref, ps_ref, (own, o1, o2, o3))


VM = pl.BlockSpec(memory_space=pltpu.VMEM)
SM = pl.BlockSpec(memory_space=pltpu.SMEM)
PARAMS = pltpu.CompilerParams(vmem_limit_bytes=VMEM_LIMIT)


def shaped(rows, cols, dtype):
    return jax.ShapeDtypeStruct((rows, cols), dtype)


def project_call(chunk, info, att, prefill_states, *weights):
    rows = pl.BlockSpec((SPLIT, BLOCK), lambda i, s: (chunk, 0))
    whole = pl.BlockSpec((SPLIT, BLOCK), lambda i, s: (0, 0))
    full = pl.BlockSpec((WIDTH, BLOCK), lambda i, s: (0, 0))
    if chunk == 0:
        kernel, extra = project_first, [pl.BlockSpec((16 * PIECE, BLOCK), lambda i, s: (0, 0))] * 2
    else:
        kernel, extra = project_second, [full]
    out_specs = [whole] * 4
    out_shape = [shaped(SPLIT, BLOCK, F32)] + [shaped(SPLIT, BLOCK, BF16)] * 3
    if chunk == 0:
        out_specs.append(full)
        out_shape.append(shaped(WIDTH, BLOCK, BF16))
    grid = pltpu.PrefetchScalarGridSpec(
        num_scalar_prefetch=1,
        grid=(1,),
        in_specs=[rows, rows] + extra,
        out_specs=out_specs,
    )
    return pl.pallas_call(
        kernel,
        grid_spec=grid,
        out_shape=out_shape,
        compiler_params=PARAMS,
        cost_estimate=pl.CostEstimate(
            flops=2 * SPLIT * BLOCK * WIDTH, transcendentals=0, bytes_accessed=6 * 1024 * 1024
        ),
    )(info, att, prefill_states, *weights)


def return_kernel(info, dec_ref, w_ref, ds_ref, out_ref, a_sc):
    head, owner = info[AT_HEAD], info[OWNER]
    shape = (256, EXTRA)
    row = lax.broadcasted_iota(jnp.int32, shape, 0)
    lane = lax.broadcasted_iota(jnp.int32, shape, 1)
    mine = jnp.full(shape, -1, jnp.int32)
    for t in range(3):
        mine = jnp.where(lane == t, info[SLOT + t], mine)
    piece, place = row >> 3, row & 7
    mask = ((piece >> 2) & 3) * 8 + (piece & 3) * 2 + (piece >> 4)
    first = (mask ^ owner) * 3
    for g in range(2):
        at = place - 3 * g
        pick = (at >= 0) & (at < 3) & (first + at == mine)
        chosen = mm(pick.astype(F32).astype(BF16), dec_ref[...], TN)
        a_sc[:, g * 2 * HEAD_SIZE : (g + 1) * 2 * HEAD_SIZE] = chosen.astype(BF16)
    part = mm(a_sc[...], w_ref[...], NT)
    for j in range(4):
        block = part[:8, j * BLOCK : (j + 1) * BLOCK]
        block = block + jnp.where(head == j, ds_ref[...].astype(F32), 0.0)
        out_ref[8 * j : 8 * j + 8, :] = block.astype(BF16)


def return_call(info, dec, w, states):
    return pl.pallas_call(
        return_kernel,
        in_specs=[SM] + [VM] * 3,
        out_specs=VM,
        out_shape=shaped(32, BLOCK, BF16),
        scratch_shapes=[pltpu.VMEM((EXTRA, BLOCK), BF16)],
        compiler_params=PARAMS,
        name="return_rows",
    )(info, dec, w, states)


def combine_kernel(info, gain_ref, *refs):
    own_ref, r1, r2, r3 = refs[-6:-2]
    summed_ref, g_ref = refs[-2:]
    total = own_ref[...] + r1[...].astype(F32) + r2[...].astype(F32) + r3[...].astype(F32)
    summed_ref[...] = total
    at = pl.multiple_of(info[AT_HEAD] * BLOCK, BLOCK)
    g_ref[:SPLIT, :] = (total * gain_ref[:, pl.ds(at, BLOCK)].astype(F32)).astype(BF16)
    if len(refs) == 7:
        g_ref[SPLIT:, :] = refs[0][...]


def combine_call(info, gain, own, parts, late=()):
    sent = SPLIT + 32 * len(late)
    return pl.pallas_call(
        combine_kernel,
        in_specs=[SM] + [VM] * (5 + len(late)),
        out_specs=[VM] * 2,
        out_shape=[shaped(SPLIT, BLOCK, F32), shaped(sent, BLOCK, BF16)],
        compiler_params=PARAMS,
    )(info, gain, *late, own, *parts)


STEP = 512
GATE_STEPS = HIDDEN // STEP


def ffn_kernel(late, info, *refs):
    parts, (gain_ref, wg, wu, wd) = refs[:4], refs[4:8]
    outs, (n_sc, r_sc, h_sc) = refs[8:12], refs[-3:]
    i = pl.program_id(0)
    head = info[AT_HEAD]

    @pl.when(i == 0)
    def _():
        squares = jnp.zeros((SPLIT, 1), F32)
        for k, part in enumerate(parts):
            at = pl.multiple_of(lax.bitwise_xor(head, k) * BLOCK, BLOCK)
            value = part[:SPLIT, :]
            n_sc[:SPLIT, pl.ds(at, BLOCK)] = value
            plain = value.astype(F32) / gain_ref[:, pl.ds(at, BLOCK)].astype(F32)
            squares = squares + jnp.sum(plain * plain, axis=1, keepdims=True)
        r_sc[:SPLIT, :] = jnp.broadcast_to(
            lax.rsqrt(squares * (1.0 / WIDTH) + norm_eps), (SPLIT, 128)
        )
        if late:
            squares = jnp.zeros((8, 1), F32)
            for j in range(4):
                rows = slice(SPLIT + 8 * j, SPLIT + 8 * j + 8)
                lanes = slice(j * BLOCK, (j + 1) * BLOCK)
                both = sum(part[rows, :].astype(F32) for part in parts)
                total = both + pltpu.roll(both, 5, 0)
                squares = squares + jnp.sum(total * total, axis=1, keepdims=True)
                scaled = total * gain_ref[:, lanes].astype(F32)
                scaled = jnp.concatenate([scaled, jnp.zeros_like(scaled)], axis=0)
                n_sc[SPLIT:, lanes] = scaled.astype(BF16)

                @pl.when(head == j)
                def _():
                    refs[12][...] = total

            scale = lax.rsqrt(squares * (1.0 / WIDTH) + norm_eps)
            r_sc[SPLIT : SPLIT + 8, :] = jnp.broadcast_to(scale, (8, 128))
            r_sc[SPLIT + 8 :, :] = jnp.zeros((8, 128), F32)

    @pl.when(i < GATE_STEPS)
    def _():
        scale = r_sc[:, :1]
        gate = mm(n_sc[...], wg[...]) * scale
        upper = mm(n_sc[...], wu[...]) * scale
        hidden = (gate / (1.0 + jnp.exp(-gate)) * upper).astype(BF16)
        h_sc[:, pl.ds(pl.multiple_of(i * STEP, STEP), STEP)] = hidden

    for k, out in enumerate(outs):

        @pl.when(i == GATE_STEPS + k)
        def _():
            out[...] = mm(h_sc[...], wd[...], NT).astype(out.dtype)


def ffn_call(late, info, parts, gain, weights):
    rows = SPLIT + EXTRA * late
    sent = SPLIT + 32 * late
    last = GATE_STEPS - 1

    def down_map(i, s):
        return (lax.bitwise_xor(s[AT_HEAD], jnp.maximum(i - GATE_STEPS, 0)), 2)

    whole = pl.BlockSpec((sent, BLOCK), lambda i, s: (0, 0))
    out = pl.BlockSpec((rows, BLOCK), lambda i, s: (0, 0))
    small = pl.BlockSpec((8, BLOCK), lambda i, s: (0, 0))
    grid = pltpu.PrefetchScalarGridSpec(
        num_scalar_prefetch=1,
        grid=(GATE_STEPS + 4,),
        in_specs=[whole] * 4
        + [
            pl.BlockSpec((1, WIDTH), lambda i, s: (0, 0)),
            pl.BlockSpec((WIDTH, STEP), lambda i, s: (0, jnp.minimum(i, last))),
            pl.BlockSpec((WIDTH, STEP), lambda i, s: (0, GATE_STEPS + jnp.minimum(i, last))),
            pl.BlockSpec((BLOCK, HIDDEN), down_map),
        ],
        out_specs=[out] * 4 + [small] * late,
        scratch_shapes=[
            pltpu.VMEM((rows, WIDTH), BF16),
            pltpu.VMEM((rows, 128), F32),
            pltpu.VMEM((rows, HIDDEN), BF16),
        ],
    )

    def kernel(*refs):
        ffn_kernel(late, *refs)

    return pl.pallas_call(
        kernel,
        grid_spec=grid,
        out_shape=[shaped(rows, BLOCK, F32)]
        + [shaped(rows, BLOCK, BF16)] * 3
        + [shaped(8, BLOCK, F32)] * late,
        compiler_params=PARAMS,
        cost_estimate=pl.CostEstimate(
            flops=6 * rows * HIDDEN * WIDTH,
            transcendentals=rows * HIDDEN,
            bytes_accessed=20 * 1024 * 1024,
        ),
    )(info, *parts, gain, weights, weights, weights)


def finish_first(s_ref, own, r1, r2, r3, p_ref):
    total = own[...] + r1[...].astype(F32) + r2[...].astype(F32) + r3[...].astype(F32)
    p_ref[...] = (s_ref[...] + total).astype(BF16)


def finish_second(old_ref, s_ref, l_ref, own, r1, r2, r3, p_ref, d_ref):
    total = own[...] + r1[...].astype(F32) + r2[...].astype(F32) + r3[...].astype(F32)
    p_ref[...] = (s_ref[...] + total[:SPLIT, :]).astype(BF16)
    d_ref[...] = (l_ref[...] + total[SPLIT : SPLIT + 8, :]).astype(BF16)[:3, :]


def finish_call(summed, own, parts, old=None, late=None):
    rows = SPLIT if old is None else SPLIT + EXTRA

    def block(n):
        return pl.BlockSpec((n, BLOCK), lambda i: (0, 0))

    first = pl.BlockSpec((SPLIT, BLOCK), lambda i: (0 if old is None else 1, 0))
    in_specs = [block(SPLIT)] + [block(rows)] * 4
    if old is None:
        return pl.pallas_call(
            finish_first,
            grid=(1,),
            in_specs=in_specs,
            out_specs=first,
            out_shape=shaped(NEW, BLOCK, BF16),
            compiler_params=PARAMS,
            name="finish_0",
        )(summed, own, *parts)
    return pl.pallas_call(
        finish_second,
        grid=(1,),
        in_specs=[pl.BlockSpec(memory_space=pl.ANY), block(SPLIT), block(8)] + [block(rows)] * 4,
        out_specs=[first, block(3)],
        out_shape=[shaped(NEW, BLOCK, BF16), shaped(3, BLOCK, BF16)],
        input_output_aliases={0: 0},
        compiler_params=PARAMS,
        name="finish_1",
    )(old, summed, late, own, *parts)


SIZE = {"x": 4, "y": 4, "core": 2, "head": 4}


def swap(value, axis, k):
    return lax.ppermute(value, axis, [(i, i ^ k) for i in range(SIZE[axis])])


def spread(value):
    for axis in ("y", "x"):
        others = [swap(value, axis, k) for k in (1, 2, 3)]
        value = jnp.concatenate([value] + others, axis=0)
    return value, swap(value, "core", 1)


def body(
    prefill_query,
    prefill_new_pairs,
    prefill_cache,
    prefill_start,
    decode_query,
    decode_fresh,
    decode_cache,
    decode_length,
    decode_slot,
    prefill_states,
    decode_states,
    output_proj,
    norm_gain,
    gate_weight,
    up_weight,
    down_weight,
):
    at = [lax.axis_index(a) for a in ("x", "y", "core", "head")]
    owner = at[0] * 8 + at[1] * 2 + at[2]
    info = jnp.concatenate(
        [prefill_start, decode_length, decode_slot, jnp.stack(at + [owner]).astype(jnp.int32)]
    )

    packed = jnp.concatenate([gate_weight, up_weight, down_weight.T], axis=1)
    weights = lax.all_gather(packed, ("x", "y", "core"), axis=0, tiled=True)

    code = decode_slot.astype(BF16)[:, None]
    unused = jnp.full((2, BLOCK), 255.0, BF16)
    piece = jnp.concatenate(
        [
            output_proj.T,
            decode_query,
            decode_fresh.reshape(3, BLOCK),
            unused,
            jnp.broadcast_to(code, (3, BLOCK)),
            jnp.broadcast_to((code + 96.0).astype(BF16), (3, BLOCK)),
            unused,
        ],
        axis=0,
    )
    piece, other = spread(piece)
    both = [v.reshape(16, PIECE, BLOCK) for v in (piece, other)]

    positions = jnp.concatenate(
        [
            prefill_start + jnp.arange(NEW, dtype=jnp.int32),
            decode_length,
            jnp.zeros((5,), jnp.int32),
        ]
    )
    cosine, sine = rope_tables(positions, HEAD_SIZE)
    fresh = prefill_new_pairs.reshape(NEW, BLOCK)
    att = prefill_call(info, prefill_query, fresh, prefill_cache, cosine, sine)
    gain = norm_gain.reshape(1, WIDTH)

    def exchanged(parts):
        return [swap(p, "head", k + 1) for k, p in enumerate(parts)]

    def shared(value):
        return [value] + [swap(value, "head", k) for k in (1, 2, 3)]

    own0, *parts0, w_all = project_call(0, info, att, prefill_states, piece, other)
    parts0 = exchanged(parts0)
    own1, *parts1 = project_call(1, info, att, prefill_states, w_all)
    parts1 = exchanged(parts1)

    decoded = decode_call(info, *both, decode_cache, cosine, sine)
    decoded = jnp.concatenate(spread(decoded), axis=0)
    states = jnp.pad(decode_states, ((3, 2), (0, 0)))
    late = return_call(info, decoded, w_all, states)

    summed0, scaled0 = combine_call(info, gain, own0, parts0)
    scaled0 = shared(scaled0)
    summed1, scaled1 = combine_call(info, gain, own1, parts1, (late,))
    scaled1 = shared(scaled1)
    own0, *parts0 = ffn_call(0, info, scaled0, gain, weights)
    parts0 = exchanged(parts0)
    own1, *parts1, late = ffn_call(1, info, scaled1, gain, weights)
    parts1 = exchanged(parts1)
    result = finish_call(summed0, own0, parts0)
    return finish_call(summed1, own1, parts1, result, late)


def solution(mesh):
    inner = Mesh(mesh.devices.reshape(4, 4, 2, 4), ("x", "y", "core", "head"))
    req = ("x", "y", "core")
    in_specs = (
        P(req, "head"),
        P(req, None, "head"),
        P(req, None, None, "head"),
        P(req),
        P(req, "head"),
        P(req, None, "head"),
        P(req, None, None, "head"),
        P(req),
        P(req),
        P(req, "head"),
        P(req, "head"),
        P("head", req),
        P(),
        P(req, "head"),
        P(req, "head"),
        P("head", req),
    )
    out_specs = (P(req, "head"), P(req, "head"))

    return jax.shard_map(body, mesh=inner, in_specs=in_specs, out_specs=out_specs, check_vma=False)
```

```python
import math

import jax
import jax.numpy as jnp
from jax import lax
from jax.experimental import pallas as pl
from jax.experimental.pallas import tpu as pltpu
from jax.sharding import Mesh
from jax.sharding import PartitionSpec as P


F32 = jnp.float32
BF16 = jnp.bfloat16
HEAD_SIZE = 128
NEW = 512
EXTRA = 16
SPLIT = 256
BLOCK = 512
WIDTH = 2048
CACHE = 2048
HIDDEN = 1536
PIECE = 80
rope_base = 1000000.0
norm_eps = 1e-06
EXP_SCALE = math.log2(math.e) / math.sqrt(HEAD_SIZE)
UNSEEN = -1e30
NT = (((1,), (1,)), ((), ()))
TN = (((0,), (0,)), ((), ()))


def limit(mib):
    return pltpu.CompilerParams(vmem_limit_bytes=mib * 1024 * 1024)


START, LENGTH, SLOT, AT_X, AT_Y, AT_CORE, AT_HEAD, OWNER = 0, 1, 4, 7, 8, 9, 10, 11


def mm(a, b, dims=(((1,), (0,)), ((), ()))):
    return lax.dot_general(a, b, dims, preferred_element_type=F32)


def rope_tables(positions, head_size):
    half_size = head_size // 2
    lane_index = jnp.arange(half_size, dtype=F32)
    inverse = jnp.power(F32(rope_base), -2.0 * lane_index / head_size)
    angles = positions.astype(F32)[:, None] * inverse[None, :]
    cosine, sine = jnp.cos(angles), jnp.sin(angles)
    return (
        jnp.concatenate([cosine, cosine], axis=1),
        jnp.concatenate([-sine, sine], axis=1),
    )


def turn(values, cosine, signed_sine):
    return values * cosine + pltpu.roll(values, HEAD_SIZE // 2, 1) * signed_sine


def prefill_kernel(info, q_ref, kf_ref, vf_ref, c_ref, cos_ref, sin_ref, o_ref, kr, qr):
    cosine, sine = cos_ref[...], sin_ref[...]
    kr[...] = turn(kf_ref[...].astype(F32), cosine, sine).astype(BF16)
    for h in range(2):
        lanes = slice(h * HEAD_SIZE, (h + 1) * HEAD_SIZE)
        qr[:, lanes] = turn(q_ref[:, lanes].astype(F32), cosine, sine).astype(BF16)
    start = info[START]

    def run(length, masked):
        old_keys = c_ref[0, 0, :length, :]
        old_values = c_ref[0, 1, :length, :]
        for r in range(NEW // SPLIT):
            seen = (r + 1) * SPLIT
            for h in range(2):
                q = qr[r * SPLIT : seen, h * HEAD_SIZE : (h + 1) * HEAD_SIZE]
                old = mm(q, old_keys, NT)
                if masked:
                    at = lax.broadcasted_iota(jnp.int32, old.shape, 1)
                    old = jnp.where(at < start, old, UNSEEN)
                new = mm(q, kr[:seen, :], NT)
                row = lax.broadcasted_iota(jnp.int32, new.shape, 0) + r * SPLIT
                col = lax.broadcasted_iota(jnp.int32, new.shape, 1)
                new = jnp.where(col <= row, new, UNSEEN)
                top = jnp.maximum(
                    jnp.max(old, axis=1, keepdims=True), jnp.max(new, axis=1, keepdims=True)
                )
                old = jnp.exp2((old - top) * EXP_SCALE)
                new = jnp.exp2((new - top) * EXP_SCALE)
                total = jnp.sum(old, axis=1, keepdims=True) + jnp.sum(new, axis=1, keepdims=True)
                blend = mm(old.astype(BF16), old_values) + mm(new.astype(BF16), vf_ref[:seen, :])
                o_ref[r * SPLIT : seen, h * HEAD_SIZE : (h + 1) * HEAD_SIZE] = (
                    blend / total
                ).astype(BF16)

    @pl.when(start >= CACHE)
    def _():
        run(CACHE, False)

    @pl.when(start < CACHE)
    def _():
        run(CACHE - NEW, True)


def prefill_call(info, query, fresh, cache, cosine, sine):
    grid = pltpu.PrefetchScalarGridSpec(
        num_scalar_prefetch=1,
        grid=(2,),
        in_specs=[
            pl.BlockSpec((NEW, 2 * HEAD_SIZE), lambda i, s: (0, i)),
            pl.BlockSpec((NEW, HEAD_SIZE), lambda i, s: (0, i)),
            pl.BlockSpec((NEW, HEAD_SIZE), lambda i, s: (0, 2 + i)),
            pl.BlockSpec((1, 2, CACHE, HEAD_SIZE), lambda i, s: (0, 0, 0, i)),
            pl.BlockSpec((NEW, HEAD_SIZE), lambda i, s: (0, 0)),
            pl.BlockSpec((NEW, HEAD_SIZE), lambda i, s: (0, 0)),
        ],
        out_specs=pl.BlockSpec((NEW, 2 * HEAD_SIZE), lambda i, s: (0, i)),
        scratch_shapes=[
            pltpu.VMEM((NEW, HEAD_SIZE), BF16),
            pltpu.VMEM((NEW, 2 * HEAD_SIZE), BF16),
        ],
    )
    return pl.pallas_call(
        prefill_kernel,
        grid_spec=grid,
        out_shape=jax.ShapeDtypeStruct((NEW, 4 * HEAD_SIZE), BF16),
        compiler_params=limit(32),
        cost_estimate=pl.CostEstimate(
            flops=4 * NEW * 4 * HEAD_SIZE * (CACHE + NEW),
            transcendentals=NEW * 4 * (CACHE + NEW),
            bytes_accessed=4 * 1024 * 1024,
        ),
        name="prefill_attention",
    )(info, query, fresh, fresh, cache, cosine, sine)


def decode_kernel(info, t0_ref, t1_ref, c_ref, cos_ref, sin_ref, o_ref, q_sc, f_sc, o_sc):
    s = pl.program_id(0)

    @pl.when(s == 0)
    def _():
        both = [r[...] for r in (t0_ref, t1_ref)]
        packed = jnp.concatenate([v[:, :8, :].reshape(128, BLOCK) for v in both], axis=0)
        code = jnp.concatenate([v[:, 8:, :128].reshape(128, 128) for v in both], axis=0)
        code = code[:, :8].astype(F32)
        want = info[OWNER] * 3 + lax.broadcasted_iota(jnp.int32, code.shape, 1)
        lane = lax.broadcasted_iota(jnp.int32, code.shape, 1)
        want = jnp.where(lane < 3, want, 1000).astype(F32)
        q = mm((code == want).astype(F32).astype(BF16), packed, TN)
        f = mm((code == want + 96.0).astype(F32).astype(BF16), packed, TN)
        cosine, sine = cos_ref[...], sin_ref[...]
        for h in range(4):
            lanes = slice(h * HEAD_SIZE, (h + 1) * HEAD_SIZE)
            q_sc[:, lanes] = turn(q[:, lanes], cosine, sine).astype(BF16).astype(F32)
            if h < 2:
                f_sc[:, lanes] = turn(f[:, lanes], cosine, sine).astype(BF16).astype(F32)
            else:
                f_sc[:, lanes] = f[:, lanes]
        o_sc[...] = jnp.zeros_like(o_sc)

    length = info[LENGTH + s]
    mine = lax.broadcasted_iota(jnp.int32, (8, BLOCK), 0) == s
    q = jnp.sum(jnp.where(mine, q_sc[...], 0.0), axis=0, keepdims=True)
    f = jnp.sum(jnp.where(mine, f_sc[...], 0.0), axis=0, keepdims=True)
    row = lax.broadcasted_iota(jnp.int32, (8, HEAD_SIZE), 0)

    def place(a, b):
        left = jnp.broadcast_to(q[:, a * HEAD_SIZE : (a + 1) * HEAD_SIZE], (8, HEAD_SIZE))
        right = jnp.broadcast_to(q[:, b * HEAD_SIZE : (b + 1) * HEAD_SIZE], (8, HEAD_SIZE))
        return jnp.where(row == a, left, jnp.where(row == b, right, 0.0))

    wide = jnp.concatenate([place(0, 1), place(2, 3)], axis=1)
    scores = mm(wide.astype(BF16), c_ref[0, 0], NT)
    at = lax.broadcasted_iota(jnp.int32, scores.shape, 1)
    scores = jnp.where(at < length, scores, UNSEEN)
    own = jnp.sum(wide * f[:, : 2 * HEAD_SIZE], axis=1, keepdims=True)
    top = jnp.maximum(jnp.max(scores, axis=1, keepdims=True), own)
    raw = jnp.exp2((scores - top) * EXP_SCALE)
    raw_own = jnp.exp2((own - top) * EXP_SCALE)
    total = jnp.sum(raw, axis=1, keepdims=True) + raw_own
    blend = mm(raw.astype(BF16), c_ref[0, 1])
    blend = blend + raw_own.astype(BF16).astype(F32) * f[:, 2 * HEAD_SIZE :]
    blend = blend / total
    upper = jnp.concatenate([blend[0:1, :HEAD_SIZE], blend[1:2, :HEAD_SIZE]], axis=1)
    lower = jnp.concatenate([blend[2:3, HEAD_SIZE:], blend[3:4, HEAD_SIZE:]], axis=1)
    row = lax.broadcasted_iota(jnp.int32, (8, 2 * HEAD_SIZE), 0)
    o_sc[...] = jnp.where(row == s, upper, jnp.where(row == s + 3, lower, o_sc[...]))

    @pl.when(s == 2)
    def _():
        o_ref[...] = o_sc[...].astype(BF16)


def decode_call(info, piece, other, cache, cosine, sine):
    grid = pltpu.PrefetchScalarGridSpec(
        num_scalar_prefetch=1,
        grid=(3,),
        in_specs=[
            pl.BlockSpec((16, 16, BLOCK), lambda i, s: (0, 4, 0)),
            pl.BlockSpec((16, 16, BLOCK), lambda i, s: (0, 4, 0)),
            pl.BlockSpec((1, 2, CACHE, 2 * HEAD_SIZE), lambda i, s: (i, 0, 0, 0)),
            pl.BlockSpec((8, HEAD_SIZE), lambda i, s: (NEW // 8, 0)),
            pl.BlockSpec((8, HEAD_SIZE), lambda i, s: (NEW // 8, 0)),
        ],
        out_specs=pl.BlockSpec((8, 2 * HEAD_SIZE), lambda i, s: (0, 0)),
        scratch_shapes=[
            pltpu.VMEM((8, 4 * HEAD_SIZE), F32),
            pltpu.VMEM((8, 4 * HEAD_SIZE), F32),
            pltpu.VMEM((8, 2 * HEAD_SIZE), F32),
        ],
    )
    return pl.pallas_call(
        decode_kernel,
        grid_spec=grid,
        out_shape=jax.ShapeDtypeStruct((8, 2 * HEAD_SIZE), BF16),
        compiler_params=limit(16),
        cost_estimate=pl.CostEstimate(
            flops=3 * 4 * 256 * CACHE * 256, transcendentals=0, bytes_accessed=7 * 1024 * 1024
        ),
        name="decode_attention",
    )(info, piece, other, cache, cosine, sine)


def project_kernel(info, a_ref, ps_ref, w0_ref, w1_ref, *outs):
    own0, own1, w_out = outs[0], outs[4], outs[8]
    x, y, core = (info[i] for i in (AT_X, AT_Y, AT_CORE))
    for xi in range(4):
        for yi in range(4):
            place = (lax.bitwise_xor(x, xi) * 4 + lax.bitwise_xor(y, yi)) * PIECE
            place = pl.multiple_of(place, 16)
            to = (xi * 8 + yi * 2) * 64

            @pl.when(core == 0)
            def _():
                w_out[to : to + 64, :] = w0_ref[pl.ds(place, 64), :]
                w_out[to + 64 : to + 128, :] = w1_ref[pl.ds(place, 64), :]

            @pl.when(core == 1)
            def _():
                w_out[to : to + 64, :] = w1_ref[pl.ds(place, 64), :]
                w_out[to + 64 : to + 128, :] = w0_ref[pl.ds(place, 64), :]

    for k in range(4):
        at = pl.multiple_of(lax.bitwise_xor(info[AT_HEAD], k) * BLOCK, BLOCK)
        part = mm(a_ref[...], w_out[pl.ds(at, BLOCK), :], NT)
        if k == 0:
            part = part + ps_ref[...].astype(F32)
            own0[...] = part[:SPLIT, :]
            own1[...] = part[SPLIT:, :]
        else:
            outs[k][...] = part[:SPLIT, :].astype(BF16)
            outs[4 + k][...] = part[SPLIT:, :].astype(BF16)


VM = pl.BlockSpec(memory_space=pltpu.VMEM)
SM = pl.BlockSpec(memory_space=pltpu.SMEM)


def shaped(rows, cols, dtype):
    return jax.ShapeDtypeStruct((rows, cols), dtype)


def project_call(info, att, prefill_states, *weights):
    half = [shaped(SPLIT, BLOCK, F32)] + [shaped(SPLIT, BLOCK, BF16)] * 3
    return pl.pallas_call(
        project_kernel,
        in_specs=[SM] + [VM] * 4,
        out_specs=[VM] * 9,
        out_shape=half + half + [shaped(WIDTH, BLOCK, BF16)],
        compiler_params=limit(20),
        cost_estimate=pl.CostEstimate(
            flops=2 * NEW * BLOCK * WIDTH, transcendentals=0, bytes_accessed=6 * 1024 * 1024
        ),
        name="project",
    )(info, att, prefill_states, *weights)


def return_kernel(info, dec_ref, w_ref, ds_ref, out_ref, a_sc):
    head, owner = info[AT_HEAD], info[OWNER]
    shape = (256, EXTRA)
    row = lax.broadcasted_iota(jnp.int32, shape, 0)
    lane = lax.broadcasted_iota(jnp.int32, shape, 1)
    mine = jnp.full(shape, -1, jnp.int32)
    for t in range(3):
        mine = jnp.where(lane == t, info[SLOT + t], mine)
    piece, place = row >> 3, row & 7
    mask = ((piece >> 2) & 3) * 8 + (piece & 3) * 2 + (piece >> 4)
    first = (mask ^ owner) * 3
    for g in range(2):
        at = place - 3 * g
        pick = (at >= 0) & (at < 3) & (first + at == mine)
        chosen = mm(pick.astype(F32).astype(BF16), dec_ref[...], TN)
        a_sc[:, g * 2 * HEAD_SIZE : (g + 1) * 2 * HEAD_SIZE] = chosen.astype(BF16)
    part = mm(a_sc[...], w_ref[...], NT)
    for j in range(4):
        block = part[:8, j * BLOCK : (j + 1) * BLOCK]
        block = block + jnp.where(head == j, ds_ref[...].astype(F32), 0.0)
        out_ref[8 * j : 8 * j + 8, :] = block.astype(BF16)


def return_call(info, dec, w, states):
    return pl.pallas_call(
        return_kernel,
        in_specs=[SM] + [VM] * 3,
        out_specs=VM,
        out_shape=shaped(32, BLOCK, BF16),
        scratch_shapes=[pltpu.VMEM((EXTRA, BLOCK), BF16)],
        compiler_params=limit(10),
        name="return_rows",
    )(info, dec, w, states)


def combine_kernel(info, gain_ref, *refs):
    own_ref, r1, r2, r3 = refs[-6:-2]
    summed_ref, g_ref = refs[-2:]
    total = own_ref[...] + r1[...].astype(F32) + r2[...].astype(F32) + r3[...].astype(F32)
    summed_ref[...] = total
    at = pl.multiple_of(info[AT_HEAD] * BLOCK, BLOCK)
    g_ref[:SPLIT, :] = (total * gain_ref[:, pl.ds(at, BLOCK)].astype(F32)).astype(BF16)
    if len(refs) == 7:
        g_ref[SPLIT:, :] = refs[0][...]


def combine_call(info, gain, own, parts, late=()):
    sent = SPLIT + 32 * len(late)
    return pl.pallas_call(
        combine_kernel,
        in_specs=[SM] + [VM] * (5 + len(late)),
        out_specs=[VM] * 2,
        out_shape=[shaped(SPLIT, BLOCK, F32), shaped(sent, BLOCK, BF16)],
        compiler_params=limit(8),
    )(info, gain, *late, own, *parts)


STEP = 256
STEPS = WIDTH // STEP


def ffn_kernel(late, info, *refs):
    parts, (gain_ref, w_ref) = refs[:4], refs[4:6]
    outs, (n_sc, r_sc, acc, d_sc, h_sc) = refs[6:10], refs[-5:]
    i = pl.program_id(0)
    head = info[AT_HEAD]

    @pl.when(i == 0)
    def _():
        squares = jnp.zeros((SPLIT, 1), F32)
        for k, part in enumerate(parts):
            at = pl.multiple_of(lax.bitwise_xor(head, k) * BLOCK, BLOCK)
            value = part[:SPLIT, :]
            n_sc[:SPLIT, pl.ds(at, BLOCK)] = value
            plain = value.astype(F32) / gain_ref[:, pl.ds(at, BLOCK)].astype(F32)
            squares = squares + jnp.sum(plain * plain, axis=1, keepdims=True)
        r_sc[:SPLIT, :] = jnp.broadcast_to(
            lax.rsqrt(squares * (1.0 / WIDTH) + norm_eps), (SPLIT, 128)
        )
        if late:
            squares = jnp.zeros((8, 1), F32)
            for j in range(4):
                rows = slice(SPLIT + 8 * j, SPLIT + 8 * j + 8)
                lanes = slice(j * BLOCK, (j + 1) * BLOCK)
                both = sum(part[rows, :].astype(F32) for part in parts)
                total = both + pltpu.roll(both, 5, 0)
                squares = squares + jnp.sum(total * total, axis=1, keepdims=True)
                scaled = total * gain_ref[:, lanes].astype(F32)
                scaled = jnp.concatenate([scaled, jnp.zeros_like(scaled)], axis=0)
                n_sc[SPLIT:, lanes] = scaled.astype(BF16)

                @pl.when(head == j)
                def _():
                    refs[10][...] = total

            scale = lax.rsqrt(squares * (1.0 / WIDTH) + norm_eps)
            r_sc[SPLIT : SPLIT + 8, :] = jnp.broadcast_to(scale, (8, 128))
            r_sc[SPLIT + 8 :, :] = jnp.zeros((8, 128), F32)

    at = pl.multiple_of(i * STEP, STEP)
    product = mm(n_sc[:, pl.ds(at, STEP)], w_ref[:, : 2 * HIDDEN])
    d_sc[pl.ds(at, STEP), :] = w_ref[:, 2 * HIDDEN :]

    @pl.when(i == 0)
    def _():
        acc[...] = product

    @pl.when(i > 0)
    def _():
        acc[...] = acc[...] + product

    @pl.when(i == STEPS - 1)
    def _():
        scale = r_sc[:, :1]
        gate = acc[:, :HIDDEN] * scale
        upper = acc[:, HIDDEN:] * scale
        h_sc[...] = (gate / (1.0 + jnp.exp(-gate)) * upper).astype(BF16)
        for k, out in enumerate(outs):
            block = pl.multiple_of(lax.bitwise_xor(head, k) * BLOCK, BLOCK)
            out[...] = mm(h_sc[...], d_sc[pl.ds(block, BLOCK), :], NT).astype(out.dtype)


def ffn_call(late, info, parts, gain, weights):
    rows = SPLIT + EXTRA * late
    sent = SPLIT + 32 * late
    whole = pl.BlockSpec((sent, BLOCK), lambda i, s: (0, 0))
    out = pl.BlockSpec((rows, BLOCK), lambda i, s: (0, 0))
    small = pl.BlockSpec((8, BLOCK), lambda i, s: (0, 0))
    grid = pltpu.PrefetchScalarGridSpec(
        num_scalar_prefetch=1,
        grid=(STEPS,),
        in_specs=[whole] * 4
        + [
            pl.BlockSpec((1, WIDTH), lambda i, s: (0, 0)),
            pl.BlockSpec((STEP, 3 * HIDDEN), lambda i, s: (i, 0)),
        ],
        out_specs=[out] * 4 + [small] * late,
        scratch_shapes=[
            pltpu.VMEM((rows, WIDTH), BF16),
            pltpu.VMEM((rows, 128), F32),
            pltpu.VMEM((rows, 2 * HIDDEN), F32),
            pltpu.VMEM((WIDTH, HIDDEN), BF16),
            pltpu.VMEM((rows, HIDDEN), BF16),
        ],
    )

    def kernel(*refs):
        ffn_kernel(late, *refs)

    return pl.pallas_call(
        kernel,
        grid_spec=grid,
        out_shape=[shaped(rows, BLOCK, F32)]
        + [shaped(rows, BLOCK, BF16)] * 3
        + [shaped(8, BLOCK, F32)] * late,
        compiler_params=limit(32),
        cost_estimate=pl.CostEstimate(
            flops=6 * rows * HIDDEN * WIDTH,
            transcendentals=rows * HIDDEN,
            bytes_accessed=20 * 1024 * 1024,
        ),
    )(info, *parts, gain, pltpu.with_memory_space_constraint(weights, pltpu.HBM))


def finish_first(s_ref, own, r1, r2, r3, p_ref):
    total = own[...] + r1[...].astype(F32) + r2[...].astype(F32) + r3[...].astype(F32)
    p_ref[...] = (s_ref[...] + total).astype(BF16)


def finish_second(old_ref, s_ref, l_ref, own, r1, r2, r3, p_ref, d_ref):
    total = own[...] + r1[...].astype(F32) + r2[...].astype(F32) + r3[...].astype(F32)
    p_ref[...] = (s_ref[...] + total[:SPLIT, :]).astype(BF16)
    d_ref[...] = (l_ref[...] + total[SPLIT : SPLIT + 8, :]).astype(BF16)[:3, :]


def finish_call(summed, own, parts, old=None, late=None):
    rows = SPLIT if old is None else SPLIT + EXTRA

    def block(n):
        return pl.BlockSpec((n, BLOCK), lambda i: (0, 0))

    first = pl.BlockSpec((SPLIT, BLOCK), lambda i: (0 if old is None else 1, 0))
    in_specs = [block(SPLIT)] + [block(rows)] * 4
    if old is None:
        return pl.pallas_call(
            finish_first,
            grid=(1,),
            in_specs=in_specs,
            out_specs=first,
            out_shape=shaped(NEW, BLOCK, BF16),
            compiler_params=limit(6),
            name="finish_0",
        )(summed, own, *parts)
    return pl.pallas_call(
        finish_second,
        grid=(1,),
        in_specs=[pl.BlockSpec(memory_space=pl.ANY), block(SPLIT), block(8)] + [block(rows)] * 4,
        out_specs=[first, block(3)],
        out_shape=[shaped(NEW, BLOCK, BF16), shaped(3, BLOCK, BF16)],
        input_output_aliases={0: 0},
        compiler_params=limit(6),
        name="finish_1",
    )(old, summed, late, own, *parts)


SIZE = {"x": 4, "y": 4, "core": 2, "head": 4}


def swap(value, axis, k):
    return lax.ppermute(value, axis, [(i, i ^ k) for i in range(SIZE[axis])])


def spread(value):
    for axis in ("y", "x"):
        value = lax.optimization_barrier(value)
        others = [swap(value, axis, k) for k in (1, 2, 3)]
        value = jnp.concatenate([value] + others, axis=0)
    value = lax.optimization_barrier(value)
    return value, swap(value, "core", 1)


def body(
    prefill_query,
    prefill_new_pairs,
    prefill_cache,
    prefill_start,
    decode_query,
    decode_fresh,
    decode_cache,
    decode_length,
    decode_slot,
    prefill_states,
    decode_states,
    output_proj,
    norm_gain,
    gate_weight,
    up_weight,
    down_weight,
):
    at = [lax.axis_index(a) for a in ("x", "y", "core", "head")]
    owner = at[0] * 8 + at[1] * 2 + at[2]
    info = jnp.concatenate(
        [prefill_start, decode_length, decode_slot, jnp.stack(at + [owner]).astype(jnp.int32)]
    )

    packed = jnp.concatenate([gate_weight, up_weight, down_weight.T], axis=1)
    weights = lax.all_gather(packed, ("x", "y", "core"), axis=0, tiled=True)

    code = decode_slot.astype(BF16)[:, None]
    unused = jnp.full((2, BLOCK), 255.0, BF16)
    piece = jnp.concatenate(
        [
            output_proj.T,
            decode_query,
            decode_fresh.reshape(3, BLOCK),
            unused,
            jnp.broadcast_to(code, (3, BLOCK)),
            jnp.broadcast_to((code + 96.0).astype(BF16), (3, BLOCK)),
            unused,
        ],
        axis=0,
    )
    piece, other = spread(piece)
    both = [v.reshape(16, PIECE, BLOCK) for v in (piece, other)]

    positions = jnp.concatenate(
        [
            prefill_start + jnp.arange(NEW, dtype=jnp.int32),
            decode_length,
            jnp.zeros((5,), jnp.int32),
        ]
    )
    cosine, sine = rope_tables(positions, HEAD_SIZE)
    fresh = prefill_new_pairs.reshape(NEW, BLOCK)
    att = prefill_call(info, prefill_query, fresh, prefill_cache, cosine, sine)
    gain = norm_gain.reshape(1, WIDTH)

    def exchanged(parts):
        return [swap(p, "head", k + 1) for k, p in enumerate(parts)]

    def shared(value):
        return [value] + [swap(value, "head", k) for k in (1, 2, 3)]

    own0, q1, q2, q3, own1, p1, p2, p3, w_all = project_call(
        info, att, prefill_states, piece, other
    )
    parts0 = exchanged([q1, q2, q3])
    parts1 = exchanged([p1, p2, p3])

    decoded = decode_call(info, *both, decode_cache, cosine, sine)
    decoded = jnp.concatenate(spread(decoded), axis=0)
    states = jnp.pad(decode_states, ((3, 2), (0, 0)))
    late = return_call(info, decoded, w_all, states)

    summed0, scaled0 = combine_call(info, gain, own0, parts0)
    scaled0 = shared(scaled0)
    summed1, scaled1 = combine_call(info, gain, own1, parts1, (late,))
    scaled1 = shared(scaled1)
    own0, *parts0 = ffn_call(0, info, scaled0, gain, weights)
    parts0 = exchanged(parts0)
    own1, *parts1, late = ffn_call(1, info, scaled1, gain, weights)
    parts1 = exchanged(parts1)
    result = finish_call(summed0, own0, parts0)
    return finish_call(summed1, own1, parts1, result, late)


def solution(mesh):
    inner = Mesh(mesh.devices.reshape(4, 4, 2, 4), ("x", "y", "core", "head"))
    req = ("x", "y", "core")
    in_specs = (
        P(req, "head"),
        P(req, None, "head"),
        P(req, None, None, "head"),
        P(req),
        P(req, "head"),
        P(req, None, "head"),
        P(req, None, None, "head"),
        P(req),
        P(req),
        P(req, "head"),
        P(req, "head"),
        P("head", req),
        P(),
        P(req, "head"),
        P(req, "head"),
        P("head", req),
    )
    out_specs = (P(req, "head"), P(req, "head"))

    return jax.shard_map(body, mesh=inner, in_specs=in_specs, out_specs=out_specs, check_vma=False)
```

```python
import math

import jax
import jax.numpy as jnp
from jax import lax
from jax.experimental import pallas as pl
from jax.experimental.pallas import tpu as pltpu
from jax.sharding import Mesh
from jax.sharding import PartitionSpec as P


F32 = jnp.float32
BF16 = jnp.bfloat16
HEAD_SIZE = 128
NEW = 512
EXTRA = 16
SPLIT = 256
BLOCK = 512
WIDTH = 2048
CACHE = 2048
HIDDEN = 1536
PIECE = 80
rope_base = 1000000.0
norm_eps = 1e-06
EXP_SCALE = math.log2(math.e) / math.sqrt(HEAD_SIZE)
UNSEEN = -1e30
NT = (((1,), (1,)), ((), ()))
TN = (((0,), (0,)), ((), ()))


def limit(mib):
    return pltpu.CompilerParams(vmem_limit_bytes=mib * 1024 * 1024)


START, LENGTH, SLOT, AT_X, AT_Y, AT_CORE, AT_HEAD, OWNER = 0, 1, 4, 7, 8, 9, 10, 11


def mm(a, b, dims=(((1,), (0,)), ((), ()))):
    return lax.dot_general(a, b, dims, preferred_element_type=F32)


def rope_tables(positions, head_size):
    half_size = head_size // 2
    lane_index = jnp.arange(half_size, dtype=F32)
    inverse = jnp.power(F32(rope_base), -2.0 * lane_index / head_size)
    angles = positions.astype(F32)[:, None] * inverse[None, :]
    cosine, sine = jnp.cos(angles), jnp.sin(angles)
    return (
        jnp.concatenate([cosine, cosine], axis=1),
        jnp.concatenate([-sine, sine], axis=1),
    )


def turn(values, cosine, signed_sine):
    return values * cosine + pltpu.roll(values, HEAD_SIZE // 2, 1) * signed_sine


def prefill_kernel(info, q_ref, kf_ref, vf_ref, c_ref, cos_ref, sin_ref, o_ref, kr, qr):
    cosine, sine = cos_ref[...], sin_ref[...]
    kr[...] = turn(kf_ref[...].astype(F32), cosine, sine).astype(BF16)
    for h in range(2):
        lanes = slice(h * HEAD_SIZE, (h + 1) * HEAD_SIZE)
        qr[:, lanes] = turn(q_ref[:, lanes].astype(F32), cosine, sine).astype(BF16)
    start = info[START]

    def run(length, masked):
        old_keys = c_ref[0, 0, :length, :]
        old_values = c_ref[0, 1, :length, :]
        for r in range(NEW // SPLIT):
            seen = (r + 1) * SPLIT
            for h in range(2):
                q = qr[r * SPLIT : seen, h * HEAD_SIZE : (h + 1) * HEAD_SIZE]
                old = mm(q, old_keys, NT)
                if masked:
                    at = lax.broadcasted_iota(jnp.int32, old.shape, 1)
                    old = jnp.where(at < start, old, UNSEEN)
                new = mm(q, kr[:seen, :], NT)
                row = lax.broadcasted_iota(jnp.int32, new.shape, 0) + r * SPLIT
                col = lax.broadcasted_iota(jnp.int32, new.shape, 1)
                new = jnp.where(col <= row, new, UNSEEN)
                top = jnp.maximum(
                    jnp.max(old, axis=1, keepdims=True), jnp.max(new, axis=1, keepdims=True)
                )
                old = jnp.exp2((old - top) * EXP_SCALE)
                new = jnp.exp2((new - top) * EXP_SCALE)
                total = jnp.sum(old, axis=1, keepdims=True) + jnp.sum(new, axis=1, keepdims=True)
                blend = mm(old.astype(BF16), old_values) + mm(new.astype(BF16), vf_ref[:seen, :])
                o_ref[r * SPLIT : seen, h * HEAD_SIZE : (h + 1) * HEAD_SIZE] = (
                    blend / total
                ).astype(BF16)

    @pl.when(start >= CACHE)
    def _():
        run(CACHE, False)

    @pl.when(start < CACHE)
    def _():
        run(CACHE - NEW, True)


def prefill_call(info, query, fresh, cache, cosine, sine):
    grid = pltpu.PrefetchScalarGridSpec(
        num_scalar_prefetch=1,
        grid=(2,),
        in_specs=[
            pl.BlockSpec((NEW, 2 * HEAD_SIZE), lambda i, s: (0, i)),
            pl.BlockSpec((NEW, HEAD_SIZE), lambda i, s: (0, i)),
            pl.BlockSpec((NEW, HEAD_SIZE), lambda i, s: (0, 2 + i)),
            pl.BlockSpec((1, 2, CACHE, HEAD_SIZE), lambda i, s: (0, 0, 0, i)),
            pl.BlockSpec((NEW, HEAD_SIZE), lambda i, s: (0, 0)),
            pl.BlockSpec((NEW, HEAD_SIZE), lambda i, s: (0, 0)),
        ],
        out_specs=pl.BlockSpec((NEW, 2 * HEAD_SIZE), lambda i, s: (0, i)),
        scratch_shapes=[
            pltpu.VMEM((NEW, HEAD_SIZE), BF16),
            pltpu.VMEM((NEW, 2 * HEAD_SIZE), BF16),
        ],
    )
    return pl.pallas_call(
        prefill_kernel,
        grid_spec=grid,
        out_shape=jax.ShapeDtypeStruct((NEW, 4 * HEAD_SIZE), BF16),
        compiler_params=limit(32),
        cost_estimate=pl.CostEstimate(
            flops=4 * NEW * 4 * HEAD_SIZE * (CACHE + NEW),
            transcendentals=NEW * 4 * (CACHE + NEW),
            bytes_accessed=4 * 1024 * 1024,
        ),
        name="prefill_attention",
    )(info, query, fresh, fresh, cache, cosine, sine)


def decode_kernel(info, t0_ref, t1_ref, c_ref, cos_ref, sin_ref, o_ref, q_sc, f_sc, o_sc):
    s = pl.program_id(0)

    @pl.when(s == 0)
    def _():
        both = [r[...] for r in (t0_ref, t1_ref)]
        packed = jnp.concatenate([v[:, :8, :].reshape(128, BLOCK) for v in both], axis=0)
        code = jnp.concatenate([v[:, 8:, :128].reshape(128, 128) for v in both], axis=0)
        code = code[:, :8].astype(F32)
        want = info[OWNER] * 3 + lax.broadcasted_iota(jnp.int32, code.shape, 1)
        lane = lax.broadcasted_iota(jnp.int32, code.shape, 1)
        want = jnp.where(lane < 3, want, 1000).astype(F32)
        q = mm((code == want).astype(F32).astype(BF16), packed, TN)
        f = mm((code == want + 96.0).astype(F32).astype(BF16), packed, TN)
        cosine, sine = cos_ref[...], sin_ref[...]
        for h in range(4):
            lanes = slice(h * HEAD_SIZE, (h + 1) * HEAD_SIZE)
            q_sc[:, lanes] = turn(q[:, lanes], cosine, sine).astype(BF16).astype(F32)
            if h < 2:
                f_sc[:, lanes] = turn(f[:, lanes], cosine, sine).astype(BF16).astype(F32)
            else:
                f_sc[:, lanes] = f[:, lanes]
        o_sc[...] = jnp.zeros_like(o_sc)

    length = info[LENGTH + s]
    mine = lax.broadcasted_iota(jnp.int32, (8, BLOCK), 0) == s
    q = jnp.sum(jnp.where(mine, q_sc[...], 0.0), axis=0, keepdims=True)
    f = jnp.sum(jnp.where(mine, f_sc[...], 0.0), axis=0, keepdims=True)
    row = lax.broadcasted_iota(jnp.int32, (8, HEAD_SIZE), 0)

    def place(a, b):
        left = jnp.broadcast_to(q[:, a * HEAD_SIZE : (a + 1) * HEAD_SIZE], (8, HEAD_SIZE))
        right = jnp.broadcast_to(q[:, b * HEAD_SIZE : (b + 1) * HEAD_SIZE], (8, HEAD_SIZE))
        return jnp.where(row == a, left, jnp.where(row == b, right, 0.0))

    wide = jnp.concatenate([place(0, 1), place(2, 3)], axis=1)
    scores = mm(wide.astype(BF16), c_ref[0, 0], NT)
    at = lax.broadcasted_iota(jnp.int32, scores.shape, 1)
    scores = jnp.where(at < length, scores, UNSEEN)
    own = jnp.sum(wide * f[:, : 2 * HEAD_SIZE], axis=1, keepdims=True)
    top = jnp.maximum(jnp.max(scores, axis=1, keepdims=True), own)
    raw = jnp.exp2((scores - top) * EXP_SCALE)
    raw_own = jnp.exp2((own - top) * EXP_SCALE)
    total = jnp.sum(raw, axis=1, keepdims=True) + raw_own
    blend = mm(raw.astype(BF16), c_ref[0, 1])
    blend = blend + raw_own.astype(BF16).astype(F32) * f[:, 2 * HEAD_SIZE :]
    blend = blend / total
    upper = jnp.concatenate([blend[0:1, :HEAD_SIZE], blend[1:2, :HEAD_SIZE]], axis=1)
    lower = jnp.concatenate([blend[2:3, HEAD_SIZE:], blend[3:4, HEAD_SIZE:]], axis=1)
    row = lax.broadcasted_iota(jnp.int32, (8, 2 * HEAD_SIZE), 0)
    o_sc[...] = jnp.where(row == s, upper, jnp.where(row == s + 3, lower, o_sc[...]))

    @pl.when(s == 2)
    def _():
        o_ref[...] = o_sc[...].astype(BF16)


def decode_call(info, piece, other, cache, cosine, sine):
    grid = pltpu.PrefetchScalarGridSpec(
        num_scalar_prefetch=1,
        grid=(3,),
        in_specs=[
            pl.BlockSpec((16, 16, BLOCK), lambda i, s: (0, 4, 0)),
            pl.BlockSpec((16, 16, BLOCK), lambda i, s: (0, 4, 0)),
            pl.BlockSpec((1, 2, CACHE, 2 * HEAD_SIZE), lambda i, s: (i, 0, 0, 0)),
            pl.BlockSpec((8, HEAD_SIZE), lambda i, s: (NEW // 8, 0)),
            pl.BlockSpec((8, HEAD_SIZE), lambda i, s: (NEW // 8, 0)),
        ],
        out_specs=pl.BlockSpec((8, 2 * HEAD_SIZE), lambda i, s: (0, 0)),
        scratch_shapes=[
            pltpu.VMEM((8, 4 * HEAD_SIZE), F32),
            pltpu.VMEM((8, 4 * HEAD_SIZE), F32),
            pltpu.VMEM((8, 2 * HEAD_SIZE), F32),
        ],
    )
    return pl.pallas_call(
        decode_kernel,
        grid_spec=grid,
        out_shape=jax.ShapeDtypeStruct((8, 2 * HEAD_SIZE), BF16),
        compiler_params=limit(16),
        cost_estimate=pl.CostEstimate(
            flops=3 * 4 * 256 * CACHE * 256, transcendentals=0, bytes_accessed=7 * 1024 * 1024
        ),
        name="decode_attention",
    )(info, piece, other, cache, cosine, sine)


def project_kernel(info, a_ref, ps_ref, w0_ref, w1_ref, *outs):
    own0, own1, w_out = outs[0], outs[4], outs[8]
    x, y, core = (info[i] for i in (AT_X, AT_Y, AT_CORE))
    for xi in range(4):
        for yi in range(4):
            place = (lax.bitwise_xor(x, xi) * 4 + lax.bitwise_xor(y, yi)) * PIECE
            place = pl.multiple_of(place, 16)
            to = (xi * 8 + yi * 2) * 64

            @pl.when(core == 0)
            def _():
                w_out[to : to + 64, :] = w0_ref[pl.ds(place, 64), :]
                w_out[to + 64 : to + 128, :] = w1_ref[pl.ds(place, 64), :]

            @pl.when(core == 1)
            def _():
                w_out[to : to + 64, :] = w1_ref[pl.ds(place, 64), :]
                w_out[to + 64 : to + 128, :] = w0_ref[pl.ds(place, 64), :]

    for k in range(4):
        at = pl.multiple_of(lax.bitwise_xor(info[AT_HEAD], k) * BLOCK, BLOCK)
        part = mm(a_ref[...], w_out[pl.ds(at, BLOCK), :], NT)
        if k == 0:
            part = part + ps_ref[...].astype(F32)
            own0[...] = part[:SPLIT, :]
            own1[...] = part[SPLIT:, :]
        else:
            outs[k][...] = part[:SPLIT, :].astype(BF16)
            outs[4 + k][...] = part[SPLIT:, :].astype(BF16)


VM = pl.BlockSpec(memory_space=pltpu.VMEM)
SM = pl.BlockSpec(memory_space=pltpu.SMEM)


def shaped(rows, cols, dtype):
    return jax.ShapeDtypeStruct((rows, cols), dtype)


def project_call(info, att, prefill_states, *weights):
    half = [shaped(SPLIT, BLOCK, F32)] + [shaped(SPLIT, BLOCK, BF16)] * 3
    return pl.pallas_call(
        project_kernel,
        in_specs=[SM] + [VM] * 4,
        out_specs=[VM] * 9,
        out_shape=half + half + [shaped(WIDTH, BLOCK, BF16)],
        compiler_params=limit(20),
        cost_estimate=pl.CostEstimate(
            flops=2 * NEW * BLOCK * WIDTH, transcendentals=0, bytes_accessed=6 * 1024 * 1024
        ),
        name="project",
    )(info, att, prefill_states, *weights)


def return_kernel(info, dec_ref, w_ref, ds_ref, out_ref, a_sc):
    head, owner = info[AT_HEAD], info[OWNER]
    shape = (256, EXTRA)
    row = lax.broadcasted_iota(jnp.int32, shape, 0)
    lane = lax.broadcasted_iota(jnp.int32, shape, 1)
    mine = jnp.full(shape, -1, jnp.int32)
    for t in range(3):
        mine = jnp.where(lane == t, info[SLOT + t], mine)
    piece, place = row >> 3, row & 7
    mask = ((piece >> 2) & 3) * 8 + (piece & 3) * 2 + (piece >> 4)
    first = (mask ^ owner) * 3
    for g in range(2):
        at = place - 3 * g
        pick = (at >= 0) & (at < 3) & (first + at == mine)
        chosen = mm(pick.astype(F32).astype(BF16), dec_ref[...], TN)
        a_sc[:, g * 2 * HEAD_SIZE : (g + 1) * 2 * HEAD_SIZE] = chosen.astype(BF16)
    part = mm(a_sc[...], w_ref[...], NT)
    for j in range(4):
        block = part[:8, j * BLOCK : (j + 1) * BLOCK]
        block = block + jnp.where(head == j, ds_ref[...].astype(F32), 0.0)
        out_ref[8 * j : 8 * j + 8, :] = block.astype(BF16)


def return_call(info, dec, w, states):
    return pl.pallas_call(
        return_kernel,
        in_specs=[SM] + [VM] * 3,
        out_specs=VM,
        out_shape=shaped(32, BLOCK, BF16),
        scratch_shapes=[pltpu.VMEM((EXTRA, BLOCK), BF16)],
        compiler_params=limit(10),
        name="return_rows",
    )(info, dec, w, states)


def combine_kernel(info, gain_ref, *refs):
    own_ref, r1, r2, r3 = refs[-6:-2]
    summed_ref, g_ref = refs[-2:]
    total = own_ref[...] + r1[...].astype(F32) + r2[...].astype(F32) + r3[...].astype(F32)
    summed_ref[...] = total
    at = pl.multiple_of(info[AT_HEAD] * BLOCK, BLOCK)
    g_ref[:SPLIT, :] = (total * gain_ref[:, pl.ds(at, BLOCK)].astype(F32)).astype(BF16)
    if len(refs) == 7:
        g_ref[SPLIT:, :] = refs[0][...]


def combine_call(info, gain, own, parts, late=()):
    sent = SPLIT + 32 * len(late)
    return pl.pallas_call(
        combine_kernel,
        in_specs=[SM] + [VM] * (5 + len(late)),
        out_specs=[VM] * 2,
        out_shape=[shaped(SPLIT, BLOCK, F32), shaped(sent, BLOCK, BF16)],
        compiler_params=limit(8),
    )(info, gain, *late, own, *parts)


STEP = 256
STEPS = WIDTH // STEP


def ffn_kernel(info, *refs):
    parts, (gain_ref, w_ref) = refs[:4], refs[4:6]
    outs, (n_sc, r_sc, acc, d_sc, h_sc) = refs[6:10], refs[-5:]
    i = pl.program_id(0)
    head = info[AT_HEAD]

    @pl.when(i == 0)
    def _():
        for k, part in enumerate(parts):
            at = pl.multiple_of(lax.bitwise_xor(head, k) * BLOCK, BLOCK)
            n_sc[:, pl.ds(at, BLOCK)] = part[...]
        r_sc[...] = jnp.zeros_like(r_sc)
        acc[...] = jnp.zeros_like(acc)

    at = pl.multiple_of(i * STEP, STEP)
    value = n_sc[:, pl.ds(at, STEP)]
    acc[...] = acc[...] + mm(value, w_ref[:, : 2 * HIDDEN])
    d_sc[pl.ds(at, STEP), :] = w_ref[:, 2 * HIDDEN :]
    plain = value.astype(F32) / gain_ref[:, pl.ds(at, STEP)].astype(F32)
    plain = plain * plain
    r_sc[...] = r_sc[...] + sum(plain[:, c : c + 128] for c in range(0, STEP, 128))

    @pl.when(i == STEPS - 1)
    def _():
        squares = jnp.sum(r_sc[...], axis=1, keepdims=True)
        scale = lax.rsqrt(squares * (1.0 / WIDTH) + norm_eps)
        gate = acc[:, :HIDDEN] * scale
        upper = acc[:, HIDDEN:] * scale
        h_sc[...] = (gate / (1.0 + jnp.exp(-gate)) * upper).astype(BF16)
        for k, out in enumerate(outs):
            block = pl.multiple_of(lax.bitwise_xor(head, k) * BLOCK, BLOCK)
            out[...] = mm(h_sc[...], d_sc[pl.ds(block, BLOCK), :], NT).astype(out.dtype)


def ffn_call(info, parts, gain, weights):
    whole = pl.BlockSpec((SPLIT, BLOCK), lambda i, s: (0, 0))
    grid = pltpu.PrefetchScalarGridSpec(
        num_scalar_prefetch=1,
        grid=(STEPS,),
        in_specs=[whole] * 4
        + [
            pl.BlockSpec((1, WIDTH), lambda i, s: (0, 0)),
            pl.BlockSpec((STEP, 3 * HIDDEN), lambda i, s: (i, 0)),
        ],
        out_specs=[whole] * 4,
        scratch_shapes=[
            pltpu.VMEM((SPLIT, WIDTH), BF16),
            pltpu.VMEM((SPLIT, 128), F32),
            pltpu.VMEM((SPLIT, 2 * HIDDEN), F32),
            pltpu.VMEM((WIDTH, HIDDEN), BF16),
            pltpu.VMEM((SPLIT, HIDDEN), BF16),
        ],
    )
    return pl.pallas_call(
        ffn_kernel,
        grid_spec=grid,
        out_shape=[shaped(SPLIT, BLOCK, F32)] + [shaped(SPLIT, BLOCK, BF16)] * 3,
        compiler_params=limit(24),
        cost_estimate=pl.CostEstimate(
            flops=6 * SPLIT * HIDDEN * WIDTH,
            transcendentals=SPLIT * HIDDEN,
            bytes_accessed=20 * 1024 * 1024,
        ),
        name="ffn",
    )(info, *parts, gain, pltpu.with_memory_space_constraint(weights, pltpu.HBM))


TILE = 512
GATE_TILES = HIDDEN // TILE


def ffn_late_kernel(info, *refs):
    parts, (gain_ref, wg, wu, wd) = refs[:4], refs[4:8]
    outs, (n_sc, r_sc, h_sc) = refs[8:12], refs[-3:]
    i = pl.program_id(0)
    head = info[AT_HEAD]

    @pl.when(i == 0)
    def _():
        squares = jnp.zeros((SPLIT, 1), F32)
        for k, part in enumerate(parts):
            at = pl.multiple_of(lax.bitwise_xor(head, k) * BLOCK, BLOCK)
            value = part[:SPLIT, :]
            n_sc[:SPLIT, pl.ds(at, BLOCK)] = value
            plain = value.astype(F32) / gain_ref[:, pl.ds(at, BLOCK)].astype(F32)
            squares = squares + jnp.sum(plain * plain, axis=1, keepdims=True)
        r_sc[:SPLIT, :] = jnp.broadcast_to(
            lax.rsqrt(squares * (1.0 / WIDTH) + norm_eps), (SPLIT, 128)
        )
        squares = jnp.zeros((8, 1), F32)
        for j in range(4):
            rows = slice(SPLIT + 8 * j, SPLIT + 8 * j + 8)
            lanes = slice(j * BLOCK, (j + 1) * BLOCK)
            both = sum(part[rows, :].astype(F32) for part in parts)
            total = both + pltpu.roll(both, 5, 0)
            squares = squares + jnp.sum(total * total, axis=1, keepdims=True)
            scaled = total * gain_ref[:, lanes].astype(F32)
            scaled = jnp.concatenate([scaled, jnp.zeros_like(scaled)], axis=0)
            n_sc[SPLIT:, lanes] = scaled.astype(BF16)

            @pl.when(head == j)
            def _():
                refs[12][...] = total

        scale = lax.rsqrt(squares * (1.0 / WIDTH) + norm_eps)
        r_sc[SPLIT : SPLIT + 8, :] = jnp.broadcast_to(scale, (8, 128))
        r_sc[SPLIT + 8 :, :] = jnp.zeros((8, 128), F32)

    @pl.when(i < GATE_TILES)
    def _():
        scale = r_sc[:, :1]
        gate = mm(n_sc[...], wg[...]) * scale
        upper = mm(n_sc[...], wu[...]) * scale
        hidden = (gate / (1.0 + jnp.exp(-gate)) * upper).astype(BF16)
        h_sc[:, pl.ds(pl.multiple_of(i * TILE, TILE), TILE)] = hidden

    for k, out in enumerate(outs):

        @pl.when(i == GATE_TILES + k)
        def _():
            out[...] = mm(h_sc[...], wd[...], NT).astype(out.dtype)


def ffn_late_call(info, parts, gain, weights):
    rows = SPLIT + EXTRA
    sent = SPLIT + 32
    last = GATE_TILES - 1

    def down_map(i, s):
        return (lax.bitwise_xor(s[AT_HEAD], jnp.maximum(i - GATE_TILES, 0)), 2)

    whole = pl.BlockSpec((sent, BLOCK), lambda i, s: (0, 0))
    out = pl.BlockSpec((rows, BLOCK), lambda i, s: (0, 0))
    small = pl.BlockSpec((8, BLOCK), lambda i, s: (0, 0))
    grid = pltpu.PrefetchScalarGridSpec(
        num_scalar_prefetch=1,
        grid=(GATE_TILES + 4,),
        in_specs=[whole] * 4
        + [
            pl.BlockSpec((1, WIDTH), lambda i, s: (0, 0)),
            pl.BlockSpec((WIDTH, TILE), lambda i, s: (0, jnp.minimum(i, last))),
            pl.BlockSpec((WIDTH, TILE), lambda i, s: (0, GATE_TILES + jnp.minimum(i, last))),
            pl.BlockSpec((BLOCK, HIDDEN), down_map),
        ],
        out_specs=[out] * 4 + [small],
        scratch_shapes=[
            pltpu.VMEM((rows, WIDTH), BF16),
            pltpu.VMEM((rows, 128), F32),
            pltpu.VMEM((rows, HIDDEN), BF16),
        ],
    )

    return pl.pallas_call(
        ffn_late_kernel,
        grid_spec=grid,
        out_shape=[shaped(rows, BLOCK, F32)]
        + [shaped(rows, BLOCK, BF16)] * 3
        + [shaped(8, BLOCK, F32)],
        compiler_params=limit(22),
        cost_estimate=pl.CostEstimate(
            flops=6 * rows * HIDDEN * WIDTH,
            transcendentals=rows * HIDDEN,
            bytes_accessed=20 * 1024 * 1024,
        ),
        name="ffn_late",
    )(info, *parts, gain, weights, weights, weights)


def finish_first(s_ref, own, r1, r2, r3, p_ref):
    total = own[...] + r1[...].astype(F32) + r2[...].astype(F32) + r3[...].astype(F32)
    p_ref[...] = (s_ref[...] + total).astype(BF16)


def finish_second(old_ref, s_ref, l_ref, own, r1, r2, r3, p_ref, d_ref):
    total = own[...] + r1[...].astype(F32) + r2[...].astype(F32) + r3[...].astype(F32)
    p_ref[...] = (s_ref[...] + total[:SPLIT, :]).astype(BF16)
    d_ref[...] = (l_ref[...] + total[SPLIT : SPLIT + 8, :]).astype(BF16)[:3, :]


def finish_call(summed, own, parts, old=None, late=None):
    rows = SPLIT if old is None else SPLIT + EXTRA

    def block(n):
        return pl.BlockSpec((n, BLOCK), lambda i: (0, 0))

    first = pl.BlockSpec((SPLIT, BLOCK), lambda i: (0 if old is None else 1, 0))
    in_specs = [block(SPLIT)] + [block(rows)] * 4
    if old is None:
        return pl.pallas_call(
            finish_first,
            grid=(1,),
            in_specs=in_specs,
            out_specs=first,
            out_shape=shaped(NEW, BLOCK, BF16),
            compiler_params=limit(6),
            name="finish_0",
        )(summed, own, *parts)
    return pl.pallas_call(
        finish_second,
        grid=(1,),
        in_specs=[pl.BlockSpec(memory_space=pl.ANY), block(SPLIT), block(8)] + [block(rows)] * 4,
        out_specs=[first, block(3)],
        out_shape=[shaped(NEW, BLOCK, BF16), shaped(3, BLOCK, BF16)],
        input_output_aliases={0: 0},
        compiler_params=limit(6),
        name="finish_1",
    )(old, summed, late, own, *parts)


SIZE = {"x": 4, "y": 4, "core": 2, "head": 4}


def swap(value, axis, k):
    return lax.ppermute(value, axis, [(i, i ^ k) for i in range(SIZE[axis])])


def spread(value):
    for axis in ("y", "x"):
        value = lax.optimization_barrier(value)
        others = [swap(value, axis, k) for k in (1, 2, 3)]
        value = jnp.concatenate([value] + others, axis=0)
    value = lax.optimization_barrier(value)
    return value, swap(value, "core", 1)


def body(
    prefill_query,
    prefill_new_pairs,
    prefill_cache,
    prefill_start,
    decode_query,
    decode_fresh,
    decode_cache,
    decode_length,
    decode_slot,
    prefill_states,
    decode_states,
    output_proj,
    norm_gain,
    gate_weight,
    up_weight,
    down_weight,
):
    at = [lax.axis_index(a) for a in ("x", "y", "core", "head")]
    owner = at[0] * 8 + at[1] * 2 + at[2]
    info = jnp.concatenate(
        [prefill_start, decode_length, decode_slot, jnp.stack(at + [owner]).astype(jnp.int32)]
    )

    packed = jnp.concatenate([gate_weight, up_weight, down_weight.T], axis=1)
    weights = lax.all_gather(packed, ("x", "y", "core"), axis=0, tiled=True)

    code = decode_slot.astype(BF16)[:, None]
    unused = jnp.full((2, BLOCK), 255.0, BF16)
    piece = jnp.concatenate(
        [
            output_proj.T,
            decode_query,
            decode_fresh.reshape(3, BLOCK),
            unused,
            jnp.broadcast_to(code, (3, BLOCK)),
            jnp.broadcast_to((code + 96.0).astype(BF16), (3, BLOCK)),
            unused,
        ],
        axis=0,
    )
    piece, other = spread(piece)
    both = [v.reshape(16, PIECE, BLOCK) for v in (piece, other)]

    positions = jnp.concatenate(
        [
            prefill_start + jnp.arange(NEW, dtype=jnp.int32),
            decode_length,
            jnp.zeros((5,), jnp.int32),
        ]
    )
    cosine, sine = rope_tables(positions, HEAD_SIZE)
    fresh = prefill_new_pairs.reshape(NEW, BLOCK)
    att = prefill_call(info, prefill_query, fresh, prefill_cache, cosine, sine)
    gain = norm_gain.reshape(1, WIDTH)

    def exchanged(parts):
        return [swap(p, "head", k + 1) for k, p in enumerate(parts)]

    def shared(value):
        return [value] + [swap(value, "head", k) for k in (1, 2, 3)]

    own0, q1, q2, q3, own1, p1, p2, p3, w_all = project_call(
        info, att, prefill_states, piece, other
    )
    parts0 = exchanged([q1, q2, q3])
    decoded = decode_call(info, *both, decode_cache, cosine, sine)
    decoded, p1, p2, p3 = lax.optimization_barrier((decoded, p1, p2, p3))
    parts1 = exchanged([p1, p2, p3])
    decoded = jnp.concatenate(spread(decoded), axis=0)
    states = jnp.pad(decode_states, ((3, 2), (0, 0)))
    late = return_call(info, decoded, w_all, states)

    summed0, scaled0 = combine_call(info, gain, own0, parts0)
    scaled0 = shared(scaled0)
    summed1, scaled1 = combine_call(info, gain, own1, parts1, (late,))
    scaled1 = shared(scaled1)
    own0, *parts0 = ffn_call(info, scaled0, gain, weights)
    parts0 = exchanged(parts0)
    own1, *parts1, late = ffn_late_call(info, scaled1, gain, weights)
    parts1 = exchanged(parts1)
    result = finish_call(summed0, own0, parts0)
    return finish_call(summed1, own1, parts1, result, late)


def solution(mesh):
    inner = Mesh(mesh.devices.reshape(4, 4, 2, 4), ("x", "y", "core", "head"))
    req = ("x", "y", "core")
    in_specs = (
        P(req, "head"),
        P(req, None, "head"),
        P(req, None, None, "head"),
        P(req),
        P(req, "head"),
        P(req, None, "head"),
        P(req, None, None, "head"),
        P(req),
        P(req),
        P(req, "head"),
        P(req, "head"),
        P("head", req),
        P(),
        P(req, "head"),
        P(req, "head"),
        P("head", req),
    )
    out_specs = (P(req, "head"), P(req, "head"))

    return jax.shard_map(body, mesh=inner, in_specs=in_specs, out_specs=out_specs, check_vma=False)
```

```python
import math

import jax
import jax.numpy as jnp
from jax import lax
from jax.experimental import pallas as pl
from jax.experimental.pallas import tpu as pltpu
from jax.sharding import Mesh
from jax.sharding import PartitionSpec as P


F32 = jnp.float32
BF16 = jnp.bfloat16
HEAD_SIZE = 128
NEW = 512
EXTRA = 16
SPLIT = 256
BLOCK = 512
WIDTH = 2048
CACHE = 2048
HIDDEN = 1536
PIECE = 80
rope_base = 1000000.0
norm_eps = 1e-06
EXP_SCALE = math.log2(math.e) / math.sqrt(HEAD_SIZE)
UNSEEN = -1e30
NT = (((1,), (1,)), ((), ()))
TN = (((0,), (0,)), ((), ()))


def limit(mib):
    return pltpu.CompilerParams(vmem_limit_bytes=mib * 1024 * 1024)


START, LENGTH, SLOT, AT_X, AT_Y, AT_CORE, AT_HEAD, OWNER = 0, 1, 4, 7, 8, 9, 10, 11


def mm(a, b, dims=(((1,), (0,)), ((), ()))):
    return lax.dot_general(a, b, dims, preferred_element_type=F32)


def rope_tables(positions, head_size):
    half_size = head_size // 2
    lane_index = jnp.arange(half_size, dtype=F32)
    inverse = jnp.power(F32(rope_base), -2.0 * lane_index / head_size)
    angles = positions.astype(F32)[:, None] * inverse[None, :]
    cosine, sine = jnp.cos(angles), jnp.sin(angles)
    return (
        jnp.concatenate([cosine, cosine], axis=1),
        jnp.concatenate([-sine, sine], axis=1),
    )


def turn(values, cosine, signed_sine):
    return values * cosine + pltpu.roll(values, HEAD_SIZE // 2, 1) * signed_sine


def prefill_kernel(info, q_ref, kf_ref, vf_ref, c_ref, cos_ref, sin_ref, o_ref, kr, qr):
    cosine, sine = cos_ref[...], sin_ref[...]
    kr[...] = turn(kf_ref[...].astype(F32), cosine, sine).astype(BF16)
    for h in range(2):
        lanes = slice(h * HEAD_SIZE, (h + 1) * HEAD_SIZE)
        qr[:, lanes] = turn(q_ref[:, lanes].astype(F32), cosine, sine).astype(BF16)
    start = info[START]

    def run(length, masked):
        old_keys = c_ref[0, 0, :length, :]
        old_values = c_ref[0, 1, :length, :]
        for r in range(NEW // SPLIT):
            seen = (r + 1) * SPLIT
            for h in range(2):
                q = qr[r * SPLIT : seen, h * HEAD_SIZE : (h + 1) * HEAD_SIZE]
                old = mm(q, old_keys, NT)
                if masked:
                    at = lax.broadcasted_iota(jnp.int32, old.shape, 1)
                    old = jnp.where(at < start, old, UNSEEN)
                new = mm(q, kr[:seen, :], NT)
                row = lax.broadcasted_iota(jnp.int32, new.shape, 0) + r * SPLIT
                col = lax.broadcasted_iota(jnp.int32, new.shape, 1)
                new = jnp.where(col <= row, new, UNSEEN)
                top = jnp.maximum(
                    jnp.max(old, axis=1, keepdims=True), jnp.max(new, axis=1, keepdims=True)
                )
                old = jnp.exp2((old - top) * EXP_SCALE)
                new = jnp.exp2((new - top) * EXP_SCALE)
                total = jnp.sum(old, axis=1, keepdims=True) + jnp.sum(new, axis=1, keepdims=True)
                blend = mm(old.astype(BF16), old_values) + mm(new.astype(BF16), vf_ref[:seen, :])
                o_ref[r * SPLIT : seen, h * HEAD_SIZE : (h + 1) * HEAD_SIZE] = (
                    blend / total
                ).astype(BF16)

    @pl.when(start >= CACHE)
    def _():
        run(CACHE, False)

    @pl.when(start < CACHE)
    def _():
        run(CACHE - NEW, True)


def prefill_call(info, query, fresh, cache, cosine, sine):
    grid = pltpu.PrefetchScalarGridSpec(
        num_scalar_prefetch=1,
        grid=(2,),
        in_specs=[
            pl.BlockSpec((NEW, 2 * HEAD_SIZE), lambda i, s: (0, i)),
            pl.BlockSpec((NEW, HEAD_SIZE), lambda i, s: (0, i)),
            pl.BlockSpec((NEW, HEAD_SIZE), lambda i, s: (0, 2 + i)),
            pl.BlockSpec((1, 2, CACHE, HEAD_SIZE), lambda i, s: (0, 0, 0, i)),
            pl.BlockSpec((NEW, HEAD_SIZE), lambda i, s: (0, 0)),
            pl.BlockSpec((NEW, HEAD_SIZE), lambda i, s: (0, 0)),
        ],
        out_specs=pl.BlockSpec((NEW, 2 * HEAD_SIZE), lambda i, s: (0, i)),
        scratch_shapes=[
            pltpu.VMEM((NEW, HEAD_SIZE), BF16),
            pltpu.VMEM((NEW, 2 * HEAD_SIZE), BF16),
        ],
    )
    return pl.pallas_call(
        prefill_kernel,
        grid_spec=grid,
        out_shape=jax.ShapeDtypeStruct((NEW, 4 * HEAD_SIZE), BF16),
        compiler_params=limit(32),
        cost_estimate=pl.CostEstimate(
            flops=4 * NEW * 4 * HEAD_SIZE * (CACHE + NEW),
            transcendentals=NEW * 4 * (CACHE + NEW),
            bytes_accessed=4 * 1024 * 1024,
        ),
        name="prefill_attention",
    )(info, query, fresh, fresh, cache, cosine, sine)


def decode_kernel(info, t0_ref, t1_ref, c_ref, cos_ref, sin_ref, o_ref, q_sc, f_sc, o_sc):
    s = pl.program_id(0)

    @pl.when(s == 0)
    def _():
        both = [r[...] for r in (t0_ref, t1_ref)]
        packed = jnp.concatenate([v[:, :8, :].reshape(128, BLOCK) for v in both], axis=0)
        code = jnp.concatenate([v[:, 8:, :128].reshape(128, 128) for v in both], axis=0)
        code = code[:, :8].astype(F32)
        want = info[OWNER] * 3 + lax.broadcasted_iota(jnp.int32, code.shape, 1)
        lane = lax.broadcasted_iota(jnp.int32, code.shape, 1)
        want = jnp.where(lane < 3, want, 1000).astype(F32)
        q = mm((code == want).astype(F32).astype(BF16), packed, TN)
        f = mm((code == want + 96.0).astype(F32).astype(BF16), packed, TN)
        cosine, sine = cos_ref[...], sin_ref[...]
        for h in range(4):
            lanes = slice(h * HEAD_SIZE, (h + 1) * HEAD_SIZE)
            q_sc[:, lanes] = turn(q[:, lanes], cosine, sine).astype(BF16).astype(F32)
            if h < 2:
                f_sc[:, lanes] = turn(f[:, lanes], cosine, sine).astype(BF16).astype(F32)
            else:
                f_sc[:, lanes] = f[:, lanes]
        o_sc[...] = jnp.zeros_like(o_sc)

    length = info[LENGTH + s]
    mine = lax.broadcasted_iota(jnp.int32, (8, BLOCK), 0) == s
    q = jnp.sum(jnp.where(mine, q_sc[...], 0.0), axis=0, keepdims=True)
    f = jnp.sum(jnp.where(mine, f_sc[...], 0.0), axis=0, keepdims=True)
    row = lax.broadcasted_iota(jnp.int32, (8, HEAD_SIZE), 0)

    def place(a, b):
        left = jnp.broadcast_to(q[:, a * HEAD_SIZE : (a + 1) * HEAD_SIZE], (8, HEAD_SIZE))
        right = jnp.broadcast_to(q[:, b * HEAD_SIZE : (b + 1) * HEAD_SIZE], (8, HEAD_SIZE))
        return jnp.where(row == a, left, jnp.where(row == b, right, 0.0))

    wide = jnp.concatenate([place(0, 1), place(2, 3)], axis=1)
    scores = mm(wide.astype(BF16), c_ref[0, 0], NT)
    at = lax.broadcasted_iota(jnp.int32, scores.shape, 1)
    scores = jnp.where(at < length, scores, UNSEEN)
    own = jnp.sum(wide * f[:, : 2 * HEAD_SIZE], axis=1, keepdims=True)
    top = jnp.maximum(jnp.max(scores, axis=1, keepdims=True), own)
    raw = jnp.exp2((scores - top) * EXP_SCALE)
    raw_own = jnp.exp2((own - top) * EXP_SCALE)
    total = jnp.sum(raw, axis=1, keepdims=True) + raw_own
    blend = mm(raw.astype(BF16), c_ref[0, 1])
    blend = blend + raw_own.astype(BF16).astype(F32) * f[:, 2 * HEAD_SIZE :]
    blend = blend / total
    upper = jnp.concatenate([blend[0:1, :HEAD_SIZE], blend[1:2, :HEAD_SIZE]], axis=1)
    lower = jnp.concatenate([blend[2:3, HEAD_SIZE:], blend[3:4, HEAD_SIZE:]], axis=1)
    row = lax.broadcasted_iota(jnp.int32, (8, 2 * HEAD_SIZE), 0)
    o_sc[...] = jnp.where(row == s, upper, jnp.where(row == s + 3, lower, o_sc[...]))

    @pl.when(s == 2)
    def _():
        o_ref[...] = o_sc[...].astype(BF16)


def decode_call(info, piece, other, cache, cosine, sine):
    grid = pltpu.PrefetchScalarGridSpec(
        num_scalar_prefetch=1,
        grid=(3,),
        in_specs=[
            pl.BlockSpec((16, 16, BLOCK), lambda i, s: (0, 4, 0)),
            pl.BlockSpec((16, 16, BLOCK), lambda i, s: (0, 4, 0)),
            pl.BlockSpec((1, 2, CACHE, 2 * HEAD_SIZE), lambda i, s: (i, 0, 0, 0)),
            pl.BlockSpec((8, HEAD_SIZE), lambda i, s: (NEW // 8, 0)),
            pl.BlockSpec((8, HEAD_SIZE), lambda i, s: (NEW // 8, 0)),
        ],
        out_specs=pl.BlockSpec((8, 2 * HEAD_SIZE), lambda i, s: (0, 0)),
        scratch_shapes=[
            pltpu.VMEM((8, 4 * HEAD_SIZE), F32),
            pltpu.VMEM((8, 4 * HEAD_SIZE), F32),
            pltpu.VMEM((8, 2 * HEAD_SIZE), F32),
        ],
    )
    return pl.pallas_call(
        decode_kernel,
        grid_spec=grid,
        out_shape=jax.ShapeDtypeStruct((8, 2 * HEAD_SIZE), BF16),
        compiler_params=limit(16),
        cost_estimate=pl.CostEstimate(
            flops=3 * 4 * 256 * CACHE * 256, transcendentals=0, bytes_accessed=7 * 1024 * 1024
        ),
        name="decode_attention",
    )(info, piece, other, cache, cosine, sine)


def project_kernel(info, a_ref, ps_ref, w0_ref, w1_ref, *outs):
    own0, own1, w_out = outs[0], outs[4], outs[8]
    x, y, core = (info[i] for i in (AT_X, AT_Y, AT_CORE))
    for xi in range(4):
        for yi in range(4):
            place = (lax.bitwise_xor(x, xi) * 4 + lax.bitwise_xor(y, yi)) * PIECE
            place = pl.multiple_of(place, 16)
            to = (xi * 8 + yi * 2) * 64

            @pl.when(core == 0)
            def _():
                w_out[to : to + 64, :] = w0_ref[pl.ds(place, 64), :]
                w_out[to + 64 : to + 128, :] = w1_ref[pl.ds(place, 64), :]

            @pl.when(core == 1)
            def _():
                w_out[to : to + 64, :] = w1_ref[pl.ds(place, 64), :]
                w_out[to + 64 : to + 128, :] = w0_ref[pl.ds(place, 64), :]

    for k in range(4):
        at = pl.multiple_of(lax.bitwise_xor(info[AT_HEAD], k) * BLOCK, BLOCK)
        part = mm(a_ref[...], w_out[pl.ds(at, BLOCK), :], NT)
        if k == 0:
            part = part + ps_ref[...].astype(F32)
            own0[...] = part[:SPLIT, :]
            own1[...] = part[SPLIT:, :]
        else:
            outs[k][...] = part[:SPLIT, :].astype(BF16)
            outs[4 + k][...] = part[SPLIT:, :].astype(BF16)


VM = pl.BlockSpec(memory_space=pltpu.VMEM)
SM = pl.BlockSpec(memory_space=pltpu.SMEM)


def shaped(rows, cols, dtype):
    return jax.ShapeDtypeStruct((rows, cols), dtype)


def project_call(info, att, prefill_states, *weights):
    half = [shaped(SPLIT, BLOCK, F32)] + [shaped(SPLIT, BLOCK, BF16)] * 3
    return pl.pallas_call(
        project_kernel,
        in_specs=[SM] + [VM] * 4,
        out_specs=[VM] * 9,
        out_shape=half + half + [shaped(WIDTH, BLOCK, BF16)],
        compiler_params=limit(20),
        cost_estimate=pl.CostEstimate(
            flops=2 * NEW * BLOCK * WIDTH, transcendentals=0, bytes_accessed=6 * 1024 * 1024
        ),
        name="project",
    )(info, att, prefill_states, *weights)


def return_kernel(info, dec_ref, w_ref, ds_ref, out_ref, a_sc):
    head, owner = info[AT_HEAD], info[OWNER]
    shape = (256, EXTRA)
    row = lax.broadcasted_iota(jnp.int32, shape, 0)
    lane = lax.broadcasted_iota(jnp.int32, shape, 1)
    mine = jnp.full(shape, -1, jnp.int32)
    for t in range(3):
        mine = jnp.where(lane == t, info[SLOT + t], mine)
    piece, place = row >> 3, row & 7
    mask = ((piece >> 2) & 3) * 8 + (piece & 3) * 2 + (piece >> 4)
    first = (mask ^ owner) * 3
    for g in range(2):
        at = place - 3 * g
        pick = (at >= 0) & (at < 3) & (first + at == mine)
        chosen = mm(pick.astype(F32).astype(BF16), dec_ref[...], TN)
        a_sc[:, g * 2 * HEAD_SIZE : (g + 1) * 2 * HEAD_SIZE] = chosen.astype(BF16)
    part = mm(a_sc[...], w_ref[...], NT)
    for j in range(4):
        block = part[:8, j * BLOCK : (j + 1) * BLOCK]
        block = block + jnp.where(head == j, ds_ref[...].astype(F32), 0.0)
        out_ref[8 * j : 8 * j + 8, :] = block.astype(BF16)


def return_call(info, dec, w, states):
    return pl.pallas_call(
        return_kernel,
        in_specs=[SM] + [VM] * 3,
        out_specs=VM,
        out_shape=shaped(32, BLOCK, BF16),
        scratch_shapes=[pltpu.VMEM((EXTRA, BLOCK), BF16)],
        compiler_params=limit(10),
        name="return_rows",
    )(info, dec, w, states)


def combine_kernel(info, gain_ref, *refs):
    own_ref, r1, r2, r3 = refs[-6:-2]
    summed_ref, g_ref = refs[-2:]
    total = own_ref[...] + r1[...].astype(F32) + r2[...].astype(F32) + r3[...].astype(F32)
    summed_ref[...] = total
    at = pl.multiple_of(info[AT_HEAD] * BLOCK, BLOCK)
    g_ref[:SPLIT, :] = (total * gain_ref[:, pl.ds(at, BLOCK)].astype(F32)).astype(BF16)
    if len(refs) == 7:
        g_ref[SPLIT:, :] = refs[0][...]


def combine_call(info, gain, own, parts, late=()):
    sent = SPLIT + 32 * len(late)
    return pl.pallas_call(
        combine_kernel,
        in_specs=[SM] + [VM] * (5 + len(late)),
        out_specs=[VM] * 2,
        out_shape=[shaped(SPLIT, BLOCK, F32), shaped(sent, BLOCK, BF16)],
        compiler_params=limit(8),
    )(info, gain, *late, own, *parts)


STEP = 512
STEPS = WIDTH // STEP


def ffn_kernel(info, *refs):
    parts, (gain_ref, w_ref) = refs[:4], refs[4:6]
    outs, (n_sc, r_sc, acc, d_sc, h_sc) = refs[6:10], refs[-5:]
    i = pl.program_id(0)
    head = info[AT_HEAD]

    @pl.when(i == 0)
    def _():
        for k, part in enumerate(parts):
            at = pl.multiple_of(lax.bitwise_xor(head, k) * BLOCK, BLOCK)
            n_sc[:, pl.ds(at, BLOCK)] = part[...]
        r_sc[...] = jnp.zeros_like(r_sc)

    at = pl.multiple_of(i * STEP, STEP)
    value = n_sc[:, pl.ds(at, STEP)]
    product = mm(value, w_ref[:, : 2 * HIDDEN])

    @pl.when(i == 0)
    def _():
        acc[...] = product

    @pl.when(i > 0)
    def _():
        acc[...] = acc[...] + product

    d_sc[pl.ds(at, STEP), :] = w_ref[:, 2 * HIDDEN :]
    plain = value.astype(F32) / gain_ref[:, pl.ds(at, STEP)].astype(F32)
    plain = plain * plain
    r_sc[...] = r_sc[...] + sum(plain[:, c : c + 128] for c in range(0, STEP, 128))

    @pl.when(i == STEPS - 1)
    def _():
        squares = jnp.sum(r_sc[...], axis=1, keepdims=True)
        scale = lax.rsqrt(squares * (1.0 / WIDTH) + norm_eps)
        gate = acc[:, :HIDDEN] * scale
        upper = acc[:, HIDDEN:] * scale
        h_sc[...] = (gate / (1.0 + jnp.exp(-gate)) * upper).astype(BF16)
        for k, out in enumerate(outs):
            block = pl.multiple_of(lax.bitwise_xor(head, k) * BLOCK, BLOCK)
            out[...] = mm(h_sc[...], d_sc[pl.ds(block, BLOCK), :], NT).astype(out.dtype)


def ffn_call(info, parts, gain, weights):
    whole = pl.BlockSpec((SPLIT, BLOCK), lambda i, s: (0, 0))
    grid = pltpu.PrefetchScalarGridSpec(
        num_scalar_prefetch=1,
        grid=(STEPS,),
        in_specs=[whole] * 4
        + [
            pl.BlockSpec((1, WIDTH), lambda i, s: (0, 0)),
            pl.BlockSpec((STEP, 3 * HIDDEN), lambda i, s: (i, 0)),
        ],
        out_specs=[whole] * 4,
        scratch_shapes=[
            pltpu.VMEM((SPLIT, WIDTH), BF16),
            pltpu.VMEM((SPLIT, 128), F32),
            pltpu.VMEM((SPLIT, 2 * HIDDEN), F32),
            pltpu.VMEM((WIDTH, HIDDEN), BF16),
            pltpu.VMEM((SPLIT, HIDDEN), BF16),
        ],
    )
    return pl.pallas_call(
        ffn_kernel,
        grid_spec=grid,
        out_shape=[shaped(SPLIT, BLOCK, F32)] + [shaped(SPLIT, BLOCK, BF16)] * 3,
        compiler_params=limit(30),
        cost_estimate=pl.CostEstimate(
            flops=6 * SPLIT * HIDDEN * WIDTH,
            transcendentals=SPLIT * HIDDEN,
            bytes_accessed=20 * 1024 * 1024,
        ),
        name="ffn",
    )(info, *parts, gain, pltpu.with_memory_space_constraint(weights, pltpu.HBM))


TILE = 512
GATE_TILES = HIDDEN // TILE


def ffn_late_kernel(info, *refs):
    parts, (gain_ref, wg, wu, wd) = refs[:4], refs[4:8]
    outs, (n_sc, r_sc, h_sc) = refs[8:12], refs[-3:]
    i = pl.program_id(0)
    head = info[AT_HEAD]

    @pl.when(i == 0)
    def _():
        squares = jnp.zeros((SPLIT, 1), F32)
        for k, part in enumerate(parts):
            at = pl.multiple_of(lax.bitwise_xor(head, k) * BLOCK, BLOCK)
            value = part[:SPLIT, :]
            n_sc[:SPLIT, pl.ds(at, BLOCK)] = value
            plain = value.astype(F32) / gain_ref[:, pl.ds(at, BLOCK)].astype(F32)
            squares = squares + jnp.sum(plain * plain, axis=1, keepdims=True)
        r_sc[:SPLIT, :] = jnp.broadcast_to(
            lax.rsqrt(squares * (1.0 / WIDTH) + norm_eps), (SPLIT, 128)
        )
        squares = jnp.zeros((8, 1), F32)
        for j in range(4):
            rows = slice(SPLIT + 8 * j, SPLIT + 8 * j + 8)
            lanes = slice(j * BLOCK, (j + 1) * BLOCK)
            both = sum(part[rows, :].astype(F32) for part in parts)
            total = both + pltpu.roll(both, 5, 0)
            squares = squares + jnp.sum(total * total, axis=1, keepdims=True)
            scaled = total * gain_ref[:, lanes].astype(F32)
            scaled = jnp.concatenate([scaled, jnp.zeros_like(scaled)], axis=0)
            n_sc[SPLIT:, lanes] = scaled.astype(BF16)

            @pl.when(head == j)
            def _():
                refs[12][...] = total

        scale = lax.rsqrt(squares * (1.0 / WIDTH) + norm_eps)
        r_sc[SPLIT : SPLIT + 8, :] = jnp.broadcast_to(scale, (8, 128))
        r_sc[SPLIT + 8 :, :] = jnp.zeros((8, 128), F32)

    @pl.when(i < GATE_TILES)
    def _():
        scale = r_sc[:, :1]
        gate = mm(n_sc[...], wg[...]) * scale
        upper = mm(n_sc[...], wu[...]) * scale
        hidden = (gate / (1.0 + jnp.exp(-gate)) * upper).astype(BF16)
        h_sc[:, pl.ds(pl.multiple_of(i * TILE, TILE), TILE)] = hidden

    for k, out in enumerate(outs):

        @pl.when(i == GATE_TILES + k)
        def _():
            out[...] = mm(h_sc[...], wd[...], NT).astype(out.dtype)


def ffn_late_call(info, parts, gain, weights):
    rows = SPLIT + EXTRA
    sent = SPLIT + 32
    last = GATE_TILES - 1

    def down_map(i, s):
        return (lax.bitwise_xor(s[AT_HEAD], jnp.maximum(i - GATE_TILES, 0)), 2)

    whole = pl.BlockSpec((sent, BLOCK), lambda i, s: (0, 0))
    out = pl.BlockSpec((rows, BLOCK), lambda i, s: (0, 0))
    small = pl.BlockSpec((8, BLOCK), lambda i, s: (0, 0))
    grid = pltpu.PrefetchScalarGridSpec(
        num_scalar_prefetch=1,
        grid=(GATE_TILES + 4,),
        in_specs=[whole] * 4
        + [
            pl.BlockSpec((1, WIDTH), lambda i, s: (0, 0)),
            pl.BlockSpec((WIDTH, TILE), lambda i, s: (0, jnp.minimum(i, last))),
            pl.BlockSpec((WIDTH, TILE), lambda i, s: (0, GATE_TILES + jnp.minimum(i, last))),
            pl.BlockSpec((BLOCK, HIDDEN), down_map),
        ],
        out_specs=[out] * 4 + [small],
        scratch_shapes=[
            pltpu.VMEM((rows, WIDTH), BF16),
            pltpu.VMEM((rows, 128), F32),
            pltpu.VMEM((rows, HIDDEN), BF16),
        ],
    )

    return pl.pallas_call(
        ffn_late_kernel,
        grid_spec=grid,
        out_shape=[shaped(rows, BLOCK, F32)]
        + [shaped(rows, BLOCK, BF16)] * 3
        + [shaped(8, BLOCK, F32)],
        compiler_params=limit(22),
        cost_estimate=pl.CostEstimate(
            flops=6 * rows * HIDDEN * WIDTH,
            transcendentals=rows * HIDDEN,
            bytes_accessed=20 * 1024 * 1024,
        ),
        name="ffn_late",
    )(info, *parts, gain, weights, weights, weights)


def finish_first(s_ref, own, r1, r2, r3, p_ref):
    total = own[...] + r1[...].astype(F32) + r2[...].astype(F32) + r3[...].astype(F32)
    p_ref[...] = (s_ref[...] + total).astype(BF16)


def finish_second(old_ref, s_ref, l_ref, own, r1, r2, r3, p_ref, d_ref):
    total = own[...] + r1[...].astype(F32) + r2[...].astype(F32) + r3[...].astype(F32)
    p_ref[...] = (s_ref[...] + total[:SPLIT, :]).astype(BF16)
    d_ref[...] = (l_ref[...] + total[SPLIT : SPLIT + 8, :]).astype(BF16)[:3, :]


def finish_call(summed, own, parts, old=None, late=None):
    rows = SPLIT if old is None else SPLIT + EXTRA

    def block(n):
        return pl.BlockSpec((n, BLOCK), lambda i: (0, 0))

    first = pl.BlockSpec((SPLIT, BLOCK), lambda i: (0 if old is None else 1, 0))
    in_specs = [block(SPLIT)] + [block(rows)] * 4
    if old is None:
        return pl.pallas_call(
            finish_first,
            grid=(1,),
            in_specs=in_specs,
            out_specs=first,
            out_shape=shaped(NEW, BLOCK, BF16),
            compiler_params=limit(6),
            name="finish_0",
        )(summed, own, *parts)
    return pl.pallas_call(
        finish_second,
        grid=(1,),
        in_specs=[pl.BlockSpec(memory_space=pl.ANY), block(SPLIT), block(8)] + [block(rows)] * 4,
        out_specs=[first, block(3)],
        out_shape=[shaped(NEW, BLOCK, BF16), shaped(3, BLOCK, BF16)],
        input_output_aliases={0: 0},
        compiler_params=limit(6),
        name="finish_1",
    )(old, summed, late, own, *parts)


SIZE = {"x": 4, "y": 4, "core": 2, "head": 4}


def swap(value, axis, k):
    return lax.ppermute(value, axis, [(i, i ^ k) for i in range(SIZE[axis])])


def spread(value):
    for axis in ("y", "x"):
        value = lax.optimization_barrier(value)
        others = [swap(value, axis, k) for k in (1, 2, 3)]
        value = jnp.concatenate([value] + others, axis=0)
    value = lax.optimization_barrier(value)
    return value, swap(value, "core", 1)


def body(
    prefill_query,
    prefill_new_pairs,
    prefill_cache,
    prefill_start,
    decode_query,
    decode_fresh,
    decode_cache,
    decode_length,
    decode_slot,
    prefill_states,
    decode_states,
    output_proj,
    norm_gain,
    gate_weight,
    up_weight,
    down_weight,
):
    at = [lax.axis_index(a) for a in ("x", "y", "core", "head")]
    owner = at[0] * 8 + at[1] * 2 + at[2]
    info = jnp.concatenate(
        [prefill_start, decode_length, decode_slot, jnp.stack(at + [owner]).astype(jnp.int32)]
    )

    packed = jnp.concatenate([gate_weight, up_weight, down_weight.T], axis=1)
    weights = lax.all_gather(packed, ("x", "y", "core"), axis=0, tiled=True)

    code = decode_slot.astype(BF16)[:, None]
    unused = jnp.full((2, BLOCK), 255.0, BF16)
    piece = jnp.concatenate(
        [
            output_proj.T,
            decode_query,
            decode_fresh.reshape(3, BLOCK),
            unused,
            jnp.broadcast_to(code, (3, BLOCK)),
            jnp.broadcast_to((code + 96.0).astype(BF16), (3, BLOCK)),
            unused,
        ],
        axis=0,
    )
    piece, other = spread(piece)
    both = [v.reshape(16, PIECE, BLOCK) for v in (piece, other)]

    positions = jnp.concatenate(
        [
            prefill_start + jnp.arange(NEW, dtype=jnp.int32),
            decode_length,
            jnp.zeros((5,), jnp.int32),
        ]
    )
    cosine, sine = rope_tables(positions, HEAD_SIZE)
    fresh = prefill_new_pairs.reshape(NEW, BLOCK)
    att = prefill_call(info, prefill_query, fresh, prefill_cache, cosine, sine)
    gain = norm_gain.reshape(1, WIDTH)

    def exchanged(parts):
        return [swap(p, "head", k + 1) for k, p in enumerate(parts)]

    def shared(value):
        return [value] + [swap(value, "head", k) for k in (1, 2, 3)]

    own0, q1, q2, q3, own1, p1, p2, p3, w_all = project_call(
        info, att, prefill_states, piece, other
    )
    parts0 = exchanged([q1, q2, q3])
    decoded = decode_call(info, *both, decode_cache, cosine, sine)
    decoded, p1, p2, p3 = lax.optimization_barrier((decoded, p1, p2, p3))
    parts1 = exchanged([p1, p2, p3])
    decoded = jnp.concatenate(spread(decoded), axis=0)
    states = jnp.pad(decode_states, ((3, 2), (0, 0)))
    late = return_call(info, decoded, w_all, states)

    summed0, scaled0 = combine_call(info, gain, own0, parts0)
    scaled0 = shared(scaled0)
    summed1, scaled1 = combine_call(info, gain, own1, parts1, (late,))
    scaled1 = shared(scaled1)
    own0, *parts0 = ffn_call(info, scaled0, gain, weights)
    parts0 = exchanged(parts0)
    own1, *parts1, late = ffn_late_call(info, scaled1, gain, weights)
    parts1 = exchanged(parts1)
    result = finish_call(summed0, own0, parts0)
    return finish_call(summed1, own1, parts1, result, late)


def solution(mesh):
    inner = Mesh(mesh.devices.reshape(4, 4, 2, 4), ("x", "y", "core", "head"))
    req = ("x", "y", "core")
    in_specs = (
        P(req, "head"),
        P(req, None, "head"),
        P(req, None, None, "head"),
        P(req),
        P(req, "head"),
        P(req, None, "head"),
        P(req, None, None, "head"),
        P(req),
        P(req),
        P(req, "head"),
        P(req, "head"),
        P("head", req),
        P(),
        P(req, "head"),
        P(req, "head"),
        P("head", req),
    )
    out_specs = (P(req, "head"), P(req, "head"))

    return jax.shard_map(body, mesh=inner, in_specs=in_specs, out_specs=out_specs, check_vma=False)
```

```python
import math

import jax
import jax.numpy as jnp
from jax import lax
from jax.experimental import pallas as pl
from jax.experimental.pallas import tpu as pltpu
from jax.sharding import Mesh
from jax.sharding import PartitionSpec as P


F32 = jnp.float32
BF16 = jnp.bfloat16
HEAD_SIZE = 128
NEW = 512
EXTRA = 16
HALF = 256
SPLIT = 320
REST = 192
BLOCK = 512
WIDTH = 2048
CACHE = 2048
HIDDEN = 1536
PIECE = 80
rope_base = 1000000.0
norm_eps = 1e-06
EXP_SCALE = math.log2(math.e) / math.sqrt(HEAD_SIZE)
UNSEEN = -1e30
NT = (((1,), (1,)), ((), ()))
TN = (((0,), (0,)), ((), ()))


def limit(mib):
    return pltpu.CompilerParams(vmem_limit_bytes=mib * 1024 * 1024)


START, LENGTH, SLOT, AT_X, AT_Y, AT_CORE, AT_HEAD, OWNER = 0, 1, 4, 7, 8, 9, 10, 11


def mm(a, b, dims=(((1,), (0,)), ((), ()))):
    return lax.dot_general(a, b, dims, preferred_element_type=F32)


def rope_tables(positions, head_size):
    half_size = head_size // 2
    lane_index = jnp.arange(half_size, dtype=F32)
    inverse = jnp.power(F32(rope_base), -2.0 * lane_index / head_size)
    angles = positions.astype(F32)[:, None] * inverse[None, :]
    cosine, sine = jnp.cos(angles), jnp.sin(angles)
    return (
        jnp.concatenate([cosine, cosine], axis=1),
        jnp.concatenate([-sine, sine], axis=1),
    )


def turn(values, cosine, signed_sine):
    return values * cosine + pltpu.roll(values, HEAD_SIZE // 2, 1) * signed_sine


def prefill_kernel(info, q_ref, kf_ref, vf_ref, c_ref, cos_ref, sin_ref, o_ref, kr, qr):
    cosine, sine = cos_ref[...], sin_ref[...]
    kr[...] = turn(kf_ref[...].astype(F32), cosine, sine).astype(BF16)
    for h in range(2):
        lanes = slice(h * HEAD_SIZE, (h + 1) * HEAD_SIZE)
        qr[:, lanes] = turn(q_ref[:, lanes].astype(F32), cosine, sine).astype(BF16)
    start = info[START]

    def run(length, masked):
        old_keys = c_ref[0, 0, :length, :]
        old_values = c_ref[0, 1, :length, :]
        for r in range(NEW // HALF):
            seen = (r + 1) * HALF
            for h in range(2):
                q = qr[r * HALF : seen, h * HEAD_SIZE : (h + 1) * HEAD_SIZE]
                old = mm(q, old_keys, NT)
                if masked:
                    at = lax.broadcasted_iota(jnp.int32, old.shape, 1)
                    old = jnp.where(at < start, old, UNSEEN)
                new = mm(q, kr[:seen, :], NT)
                row = lax.broadcasted_iota(jnp.int32, new.shape, 0) + r * HALF
                col = lax.broadcasted_iota(jnp.int32, new.shape, 1)
                new = jnp.where(col <= row, new, UNSEEN)
                top = jnp.maximum(
                    jnp.max(old, axis=1, keepdims=True), jnp.max(new, axis=1, keepdims=True)
                )
                old = jnp.exp2((old - top) * EXP_SCALE)
                new = jnp.exp2((new - top) * EXP_SCALE)
                total = jnp.sum(old, axis=1, keepdims=True) + jnp.sum(new, axis=1, keepdims=True)
                blend = mm(old.astype(BF16), old_values) + mm(new.astype(BF16), vf_ref[:seen, :])
                o_ref[r * HALF : seen, h * HEAD_SIZE : (h + 1) * HEAD_SIZE] = (
                    blend / total
                ).astype(BF16)

    @pl.when(start >= CACHE)
    def _():
        run(CACHE, False)

    @pl.when(start < CACHE)
    def _():
        run(CACHE - NEW, True)


def prefill_call(info, query, fresh, cache, cosine, sine):
    grid = pltpu.PrefetchScalarGridSpec(
        num_scalar_prefetch=1,
        grid=(2,),
        in_specs=[
            pl.BlockSpec((NEW, 2 * HEAD_SIZE), lambda i, s: (0, i)),
            pl.BlockSpec((NEW, HEAD_SIZE), lambda i, s: (0, i)),
            pl.BlockSpec((NEW, HEAD_SIZE), lambda i, s: (0, 2 + i)),
            pl.BlockSpec((1, 2, CACHE, HEAD_SIZE), lambda i, s: (0, 0, 0, i)),
            pl.BlockSpec((NEW, HEAD_SIZE), lambda i, s: (0, 0)),
            pl.BlockSpec((NEW, HEAD_SIZE), lambda i, s: (0, 0)),
        ],
        out_specs=pl.BlockSpec((NEW, 2 * HEAD_SIZE), lambda i, s: (0, i)),
        scratch_shapes=[
            pltpu.VMEM((NEW, HEAD_SIZE), BF16),
            pltpu.VMEM((NEW, 2 * HEAD_SIZE), BF16),
        ],
    )
    return pl.pallas_call(
        prefill_kernel,
        grid_spec=grid,
        out_shape=jax.ShapeDtypeStruct((NEW, 4 * HEAD_SIZE), BF16),
        compiler_params=limit(32),
        cost_estimate=pl.CostEstimate(
            flops=4 * NEW * 4 * HEAD_SIZE * (CACHE + NEW),
            transcendentals=NEW * 4 * (CACHE + NEW),
            bytes_accessed=4 * 1024 * 1024,
        ),
        name="prefill_attention",
    )(info, query, fresh, fresh, cache, cosine, sine)


def decode_kernel(info, t0_ref, t1_ref, c_ref, cos_ref, sin_ref, o_ref, q_sc, f_sc, o_sc):
    s = pl.program_id(0)

    @pl.when(s == 0)
    def _():
        both = [r[...] for r in (t0_ref, t1_ref)]
        packed = jnp.concatenate([v[:, :8, :].reshape(128, BLOCK) for v in both], axis=0)
        code = jnp.concatenate([v[:, 8:, :128].reshape(128, 128) for v in both], axis=0)
        code = code[:, :8].astype(F32)
        want = info[OWNER] * 3 + lax.broadcasted_iota(jnp.int32, code.shape, 1)
        lane = lax.broadcasted_iota(jnp.int32, code.shape, 1)
        want = jnp.where(lane < 3, want, 1000).astype(F32)
        q = mm((code == want).astype(F32).astype(BF16), packed, TN)
        f = mm((code == want + 96.0).astype(F32).astype(BF16), packed, TN)
        cosine, sine = cos_ref[...], sin_ref[...]
        for h in range(4):
            lanes = slice(h * HEAD_SIZE, (h + 1) * HEAD_SIZE)
            q_sc[:, lanes] = turn(q[:, lanes], cosine, sine).astype(BF16).astype(F32)
            if h < 2:
                f_sc[:, lanes] = turn(f[:, lanes], cosine, sine).astype(BF16).astype(F32)
            else:
                f_sc[:, lanes] = f[:, lanes]
        o_sc[...] = jnp.zeros_like(o_sc)

    length = info[LENGTH + s]
    mine = lax.broadcasted_iota(jnp.int32, (8, BLOCK), 0) == s
    q = jnp.sum(jnp.where(mine, q_sc[...], 0.0), axis=0, keepdims=True)
    f = jnp.sum(jnp.where(mine, f_sc[...], 0.0), axis=0, keepdims=True)
    row = lax.broadcasted_iota(jnp.int32, (8, HEAD_SIZE), 0)

    def place(a, b):
        left = jnp.broadcast_to(q[:, a * HEAD_SIZE : (a + 1) * HEAD_SIZE], (8, HEAD_SIZE))
        right = jnp.broadcast_to(q[:, b * HEAD_SIZE : (b + 1) * HEAD_SIZE], (8, HEAD_SIZE))
        return jnp.where(row == a, left, jnp.where(row == b, right, 0.0))

    wide = jnp.concatenate([place(0, 1), place(2, 3)], axis=1)
    scores = mm(wide.astype(BF16), c_ref[0, 0], NT)
    at = lax.broadcasted_iota(jnp.int32, scores.shape, 1)
    scores = jnp.where(at < length, scores, UNSEEN)
    own = jnp.sum(wide * f[:, : 2 * HEAD_SIZE], axis=1, keepdims=True)
    top = jnp.maximum(jnp.max(scores, axis=1, keepdims=True), own)
    raw = jnp.exp2((scores - top) * EXP_SCALE)
    raw_own = jnp.exp2((own - top) * EXP_SCALE)
    total = jnp.sum(raw, axis=1, keepdims=True) + raw_own
    blend = mm(raw.astype(BF16), c_ref[0, 1])
    blend = blend + raw_own.astype(BF16).astype(F32) * f[:, 2 * HEAD_SIZE :]
    blend = blend / total
    upper = jnp.concatenate([blend[0:1, :HEAD_SIZE], blend[1:2, :HEAD_SIZE]], axis=1)
    lower = jnp.concatenate([blend[2:3, HEAD_SIZE:], blend[3:4, HEAD_SIZE:]], axis=1)
    row = lax.broadcasted_iota(jnp.int32, (8, 2 * HEAD_SIZE), 0)
    o_sc[...] = jnp.where(row == s, upper, jnp.where(row == s + 3, lower, o_sc[...]))

    @pl.when(s == 2)
    def _():
        o_ref[...] = o_sc[...].astype(BF16)


def decode_call(info, piece, other, cache, cosine, sine):
    grid = pltpu.PrefetchScalarGridSpec(
        num_scalar_prefetch=1,
        grid=(3,),
        in_specs=[
            pl.BlockSpec((16, 16, BLOCK), lambda i, s: (0, 4, 0)),
            pl.BlockSpec((16, 16, BLOCK), lambda i, s: (0, 4, 0)),
            pl.BlockSpec((1, 2, CACHE, 2 * HEAD_SIZE), lambda i, s: (i, 0, 0, 0)),
            pl.BlockSpec((8, HEAD_SIZE), lambda i, s: (NEW // 8, 0)),
            pl.BlockSpec((8, HEAD_SIZE), lambda i, s: (NEW // 8, 0)),
        ],
        out_specs=pl.BlockSpec((8, 2 * HEAD_SIZE), lambda i, s: (0, 0)),
        scratch_shapes=[
            pltpu.VMEM((8, 4 * HEAD_SIZE), F32),
            pltpu.VMEM((8, 4 * HEAD_SIZE), F32),
            pltpu.VMEM((8, 2 * HEAD_SIZE), F32),
        ],
    )
    return pl.pallas_call(
        decode_kernel,
        grid_spec=grid,
        out_shape=jax.ShapeDtypeStruct((8, 2 * HEAD_SIZE), BF16),
        compiler_params=limit(16),
        cost_estimate=pl.CostEstimate(
            flops=3 * 4 * 256 * CACHE * 256, transcendentals=0, bytes_accessed=7 * 1024 * 1024
        ),
        name="decode_attention",
    )(info, piece, other, cache, cosine, sine)


def project_kernel(info, a_ref, ps_ref, w0_ref, w1_ref, *outs):
    own0, own1, w_out = outs[0], outs[4], outs[8]
    x, y, core = (info[i] for i in (AT_X, AT_Y, AT_CORE))
    for xi in range(4):
        for yi in range(4):
            place = (lax.bitwise_xor(x, xi) * 4 + lax.bitwise_xor(y, yi)) * PIECE
            place = pl.multiple_of(place, 16)
            to = (xi * 8 + yi * 2) * 64

            @pl.when(core == 0)
            def _():
                w_out[to : to + 64, :] = w0_ref[pl.ds(place, 64), :]
                w_out[to + 64 : to + 128, :] = w1_ref[pl.ds(place, 64), :]

            @pl.when(core == 1)
            def _():
                w_out[to : to + 64, :] = w1_ref[pl.ds(place, 64), :]
                w_out[to + 64 : to + 128, :] = w0_ref[pl.ds(place, 64), :]

    for k in range(4):
        at = pl.multiple_of(lax.bitwise_xor(info[AT_HEAD], k) * BLOCK, BLOCK)
        part = mm(a_ref[...], w_out[pl.ds(at, BLOCK), :], NT)
        if k == 0:
            part = part + ps_ref[...].astype(F32)
            own0[...] = part[:SPLIT, :]
            own1[...] = part[SPLIT:, :]
        else:
            outs[k][...] = part[:SPLIT, :].astype(BF16)
            outs[4 + k][...] = part[SPLIT:, :].astype(BF16)


VM = pl.BlockSpec(memory_space=pltpu.VMEM)
SM = pl.BlockSpec(memory_space=pltpu.SMEM)


def shaped(rows, cols, dtype):
    return jax.ShapeDtypeStruct((rows, cols), dtype)


def project_call(info, att, prefill_states, *weights):
    shapes = []
    for rows in (SPLIT, REST):
        shapes += [shaped(rows, BLOCK, F32)] + [shaped(rows, BLOCK, BF16)] * 3
    return pl.pallas_call(
        project_kernel,
        in_specs=[SM] + [VM] * 4,
        out_specs=[VM] * 9,
        out_shape=shapes + [shaped(WIDTH, BLOCK, BF16)],
        compiler_params=limit(20),
        cost_estimate=pl.CostEstimate(
            flops=2 * NEW * BLOCK * WIDTH, transcendentals=0, bytes_accessed=6 * 1024 * 1024
        ),
        name="project",
    )(info, att, prefill_states, *weights)


def return_kernel(info, dec_ref, w_ref, ds_ref, out_ref, a_sc):
    head, owner = info[AT_HEAD], info[OWNER]
    shape = (256, EXTRA)
    row = lax.broadcasted_iota(jnp.int32, shape, 0)
    lane = lax.broadcasted_iota(jnp.int32, shape, 1)
    mine = jnp.full(shape, -1, jnp.int32)
    for t in range(3):
        mine = jnp.where(lane == t, info[SLOT + t], mine)
    piece, place = row >> 3, row & 7
    mask = ((piece >> 2) & 3) * 8 + (piece & 3) * 2 + (piece >> 4)
    first = (mask ^ owner) * 3
    for g in range(2):
        at = place - 3 * g
        pick = (at >= 0) & (at < 3) & (first + at == mine)
        chosen = mm(pick.astype(F32).astype(BF16), dec_ref[...], TN)
        a_sc[:, g * 2 * HEAD_SIZE : (g + 1) * 2 * HEAD_SIZE] = chosen.astype(BF16)
    part = mm(a_sc[...], w_ref[...], NT)
    for j in range(4):
        block = part[:8, j * BLOCK : (j + 1) * BLOCK]
        block = block + jnp.where(head == j, ds_ref[...].astype(F32), 0.0)
        out_ref[8 * j : 8 * j + 8, :] = block.astype(BF16)


def return_call(info, dec, w, states):
    return pl.pallas_call(
        return_kernel,
        in_specs=[SM] + [VM] * 3,
        out_specs=VM,
        out_shape=shaped(32, BLOCK, BF16),
        scratch_shapes=[pltpu.VMEM((EXTRA, BLOCK), BF16)],
        compiler_params=limit(10),
        name="return_rows",
    )(info, dec, w, states)


def combine_kernel(info, gain_ref, *refs):
    own_ref, r1, r2, r3 = refs[-6:-2]
    summed_ref, g_ref = refs[-2:]
    total = own_ref[...] + r1[...].astype(F32) + r2[...].astype(F32) + r3[...].astype(F32)
    summed_ref[...] = total
    at = pl.multiple_of(info[AT_HEAD] * BLOCK, BLOCK)
    rows = own_ref.shape[0]
    g_ref[:rows, :] = (total * gain_ref[:, pl.ds(at, BLOCK)].astype(F32)).astype(BF16)
    if len(refs) == 7:
        g_ref[rows:, :] = refs[0][...]


def combine_call(info, gain, own, parts, late=()):
    rows = own.shape[0]
    return pl.pallas_call(
        combine_kernel,
        in_specs=[SM] + [VM] * (5 + len(late)),
        out_specs=[VM] * 2,
        out_shape=[shaped(rows, BLOCK, F32), shaped(rows + 32 * len(late), BLOCK, BF16)],
        compiler_params=limit(10),
    )(info, gain, *late, own, *parts)


STEP = 512
STEPS = WIDTH // STEP


def ffn_kernel(info, *refs):
    parts, (gain_ref, w_ref) = refs[:4], refs[4:6]
    outs, (n_sc, r_sc, acc, d_sc, h_sc) = refs[6:10], refs[-5:]
    i = pl.program_id(0)
    head = info[AT_HEAD]

    @pl.when(i == 0)
    def _():
        for k, part in enumerate(parts):
            at = pl.multiple_of(lax.bitwise_xor(head, k) * BLOCK, BLOCK)
            n_sc[:, pl.ds(at, BLOCK)] = part[...]
        r_sc[...] = jnp.zeros_like(r_sc)

    at = pl.multiple_of(i * STEP, STEP)
    value = n_sc[:, pl.ds(at, STEP)]
    product = mm(value, w_ref[:, : 2 * HIDDEN])

    @pl.when(i == 0)
    def _():
        acc[...] = product

    @pl.when(i > 0)
    def _():
        acc[...] = acc[...] + product

    d_sc[pl.ds(at, STEP), :] = w_ref[:, 2 * HIDDEN :]
    plain = value.astype(F32) / gain_ref[:, pl.ds(at, STEP)].astype(F32)
    plain = plain * plain
    r_sc[...] = r_sc[...] + sum(plain[:, c : c + 128] for c in range(0, STEP, 128))

    @pl.when(i == STEPS - 1)
    def _():
        squares = jnp.sum(r_sc[...], axis=1, keepdims=True)
        scale = lax.rsqrt(squares * (1.0 / WIDTH) + norm_eps)
        gate = acc[:, :HIDDEN] * scale
        upper = acc[:, HIDDEN:] * scale
        h_sc[...] = (gate / (1.0 + jnp.exp(-gate)) * upper).astype(BF16)
        for k, out in enumerate(outs):
            block = pl.multiple_of(lax.bitwise_xor(head, k) * BLOCK, BLOCK)
            out[...] = mm(h_sc[...], d_sc[pl.ds(block, BLOCK), :], NT).astype(out.dtype)


def ffn_call(info, parts, gain, weights):
    whole = pl.BlockSpec((SPLIT, BLOCK), lambda i, s: (0, 0))
    grid = pltpu.PrefetchScalarGridSpec(
        num_scalar_prefetch=1,
        grid=(STEPS,),
        in_specs=[whole] * 4
        + [
            pl.BlockSpec((1, WIDTH), lambda i, s: (0, 0)),
            pl.BlockSpec((STEP, 3 * HIDDEN), lambda i, s: (i, 0)),
        ],
        out_specs=[whole] * 4,
        scratch_shapes=[
            pltpu.VMEM((SPLIT, WIDTH), BF16),
            pltpu.VMEM((SPLIT, 128), F32),
            pltpu.VMEM((SPLIT, 2 * HIDDEN), F32),
            pltpu.VMEM((WIDTH, HIDDEN), BF16),
            pltpu.VMEM((SPLIT, HIDDEN), BF16),
        ],
    )
    return pl.pallas_call(
        ffn_kernel,
        grid_spec=grid,
        out_shape=[shaped(SPLIT, BLOCK, F32)] + [shaped(SPLIT, BLOCK, BF16)] * 3,
        compiler_params=limit(32),
        cost_estimate=pl.CostEstimate(
            flops=6 * SPLIT * HIDDEN * WIDTH,
            transcendentals=SPLIT * HIDDEN,
            bytes_accessed=20 * 1024 * 1024,
        ),
        name="ffn",
    )(info, *parts, gain, pltpu.with_memory_space_constraint(weights, pltpu.HBM))


TILE = 512
GATE_TILES = HIDDEN // TILE


def ffn_late_kernel(info, *refs):
    parts, (gain_ref, wg, wu, wd) = refs[:4], refs[4:8]
    outs, (n_sc, r_sc, h_sc) = refs[8:12], refs[-3:]
    i = pl.program_id(0)
    head = info[AT_HEAD]

    @pl.when(i == 0)
    def _():
        squares = jnp.zeros((REST, 1), F32)
        for k, part in enumerate(parts):
            at = pl.multiple_of(lax.bitwise_xor(head, k) * BLOCK, BLOCK)
            value = part[:REST, :]
            n_sc[:REST, pl.ds(at, BLOCK)] = value
            plain = value.astype(F32) / gain_ref[:, pl.ds(at, BLOCK)].astype(F32)
            squares = squares + jnp.sum(plain * plain, axis=1, keepdims=True)
        r_sc[:REST, :] = jnp.broadcast_to(
            lax.rsqrt(squares * (1.0 / WIDTH) + norm_eps), (REST, 128)
        )
        squares = jnp.zeros((8, 1), F32)
        for j in range(4):
            rows = slice(REST + 8 * j, REST + 8 * j + 8)
            lanes = slice(j * BLOCK, (j + 1) * BLOCK)
            both = sum(part[rows, :].astype(F32) for part in parts)
            total = both + pltpu.roll(both, 5, 0)
            squares = squares + jnp.sum(total * total, axis=1, keepdims=True)
            scaled = total * gain_ref[:, lanes].astype(F32)
            scaled = jnp.concatenate([scaled, jnp.zeros_like(scaled)], axis=0)
            n_sc[REST:, lanes] = scaled.astype(BF16)

            @pl.when(head == j)
            def _():
                refs[12][...] = total

        scale = lax.rsqrt(squares * (1.0 / WIDTH) + norm_eps)
        r_sc[REST : REST + 8, :] = jnp.broadcast_to(scale, (8, 128))
        r_sc[REST + 8 :, :] = jnp.zeros((8, 128), F32)

    @pl.when(i < GATE_TILES)
    def _():
        scale = r_sc[:, :1]
        gate = mm(n_sc[...], wg[...]) * scale
        upper = mm(n_sc[...], wu[...]) * scale
        hidden = (gate / (1.0 + jnp.exp(-gate)) * upper).astype(BF16)
        h_sc[:, pl.ds(pl.multiple_of(i * TILE, TILE), TILE)] = hidden

    for k, out in enumerate(outs):

        @pl.when(i == GATE_TILES + k)
        def _():
            out[...] = mm(h_sc[...], wd[...], NT).astype(out.dtype)


def ffn_late_call(info, parts, gain, weights):
    rows = REST + EXTRA
    sent = REST + 32
    last = GATE_TILES - 1

    def down_map(i, s):
        return (lax.bitwise_xor(s[AT_HEAD], jnp.maximum(i - GATE_TILES, 0)), 2)

    whole = pl.BlockSpec((sent, BLOCK), lambda i, s: (0, 0))
    out = pl.BlockSpec((rows, BLOCK), lambda i, s: (0, 0))
    small = pl.BlockSpec((8, BLOCK), lambda i, s: (0, 0))
    grid = pltpu.PrefetchScalarGridSpec(
        num_scalar_prefetch=1,
        grid=(GATE_TILES + 4,),
        in_specs=[whole] * 4
        + [
            pl.BlockSpec((1, WIDTH), lambda i, s: (0, 0)),
            pl.BlockSpec((WIDTH, TILE), lambda i, s: (0, jnp.minimum(i, last))),
            pl.BlockSpec((WIDTH, TILE), lambda i, s: (0, GATE_TILES + jnp.minimum(i, last))),
            pl.BlockSpec((BLOCK, HIDDEN), down_map),
        ],
        out_specs=[out] * 4 + [small],
        scratch_shapes=[
            pltpu.VMEM((rows, WIDTH), BF16),
            pltpu.VMEM((rows, 128), F32),
            pltpu.VMEM((rows, HIDDEN), BF16),
        ],
    )

    return pl.pallas_call(
        ffn_late_kernel,
        grid_spec=grid,
        out_shape=[shaped(rows, BLOCK, F32)]
        + [shaped(rows, BLOCK, BF16)] * 3
        + [shaped(8, BLOCK, F32)],
        compiler_params=limit(22),
        cost_estimate=pl.CostEstimate(
            flops=6 * rows * HIDDEN * WIDTH,
            transcendentals=rows * HIDDEN,
            bytes_accessed=20 * 1024 * 1024,
        ),
        name="ffn_late",
    )(info, *parts, gain, weights, weights, weights)


def finish_first(s_ref, own, r1, r2, r3, p_ref):
    total = own[...] + r1[...].astype(F32) + r2[...].astype(F32) + r3[...].astype(F32)
    p_ref[...] = (s_ref[...] + total).astype(BF16)


def finish_second(old_ref, s_ref, l_ref, own, r1, r2, r3, p_ref, d_ref):
    total = own[...] + r1[...].astype(F32) + r2[...].astype(F32) + r3[...].astype(F32)
    p_ref[:SPLIT, :] = old_ref[...]
    p_ref[SPLIT:, :] = (s_ref[...] + total[:REST, :]).astype(BF16)
    d_ref[...] = (l_ref[...] + total[REST : REST + 8, :]).astype(BF16)[:3, :]


def finish_call(summed, own, parts, old=None, late=None):
    if old is None:
        return pl.pallas_call(
            finish_first,
            in_specs=[VM] * 5,
            out_specs=VM,
            out_shape=shaped(SPLIT, BLOCK, BF16),
            compiler_params=limit(6),
            name="finish_0",
        )(summed, own, *parts)
    return pl.pallas_call(
        finish_second,
        in_specs=[VM] * 7,
        out_specs=[VM] * 2,
        out_shape=[shaped(NEW, BLOCK, BF16), shaped(3, BLOCK, BF16)],
        compiler_params=limit(6),
        name="finish_1",
    )(old, summed, late, own, *parts)


SIZE = {"x": 4, "y": 4, "core": 2, "head": 4}


def swap(value, axis, k):
    return lax.ppermute(value, axis, [(i, i ^ k) for i in range(SIZE[axis])])


def spread(value):
    for axis in ("y", "x"):
        value = lax.optimization_barrier(value)
        others = [swap(value, axis, k) for k in (1, 2, 3)]
        value = jnp.concatenate([value] + others, axis=0)
    value = lax.optimization_barrier(value)
    return value, swap(value, "core", 1)


def body(
    prefill_query,
    prefill_new_pairs,
    prefill_cache,
    prefill_start,
    decode_query,
    decode_fresh,
    decode_cache,
    decode_length,
    decode_slot,
    prefill_states,
    decode_states,
    output_proj,
    norm_gain,
    gate_weight,
    up_weight,
    down_weight,
):
    at = [lax.axis_index(a) for a in ("x", "y", "core", "head")]
    owner = at[0] * 8 + at[1] * 2 + at[2]
    info = jnp.concatenate(
        [prefill_start, decode_length, decode_slot, jnp.stack(at + [owner]).astype(jnp.int32)]
    )

    packed = jnp.concatenate([gate_weight, up_weight, down_weight.T], axis=1)
    weights = lax.all_gather(packed, ("x", "y", "core"), axis=0, tiled=True)

    code = decode_slot.astype(BF16)[:, None]
    unused = jnp.full((2, BLOCK), 255.0, BF16)
    piece = jnp.concatenate(
        [
            output_proj.T,
            decode_query,
            decode_fresh.reshape(3, BLOCK),
            unused,
            jnp.broadcast_to(code, (3, BLOCK)),
            jnp.broadcast_to((code + 96.0).astype(BF16), (3, BLOCK)),
            unused,
        ],
        axis=0,
    )
    piece, other = spread(piece)
    both = [v.reshape(16, PIECE, BLOCK) for v in (piece, other)]

    positions = jnp.concatenate(
        [
            prefill_start + jnp.arange(NEW, dtype=jnp.int32),
            decode_length,
            jnp.zeros((5,), jnp.int32),
        ]
    )
    cosine, sine = rope_tables(positions, HEAD_SIZE)
    fresh = prefill_new_pairs.reshape(NEW, BLOCK)
    att = prefill_call(info, prefill_query, fresh, prefill_cache, cosine, sine)
    gain = norm_gain.reshape(1, WIDTH)

    def exchanged(parts):
        return [swap(p, "head", k + 1) for k, p in enumerate(parts)]

    def shared(value):
        return [value] + [swap(value, "head", k) for k in (1, 2, 3)]

    own0, q1, q2, q3, own1, p1, p2, p3, w_all = project_call(
        info, att, prefill_states, piece, other
    )
    parts0 = exchanged([q1, q2, q3])
    decoded = decode_call(info, *both, decode_cache, cosine, sine)
    decoded, p1, p2, p3 = lax.optimization_barrier((decoded, p1, p2, p3))
    parts1 = exchanged([p1, p2, p3])
    decoded = jnp.concatenate(spread(decoded), axis=0)
    states = jnp.pad(decode_states, ((3, 2), (0, 0)))
    late = return_call(info, decoded, w_all, states)

    summed0, scaled0 = combine_call(info, gain, own0, parts0)
    scaled0 = shared(scaled0)
    summed1, scaled1 = combine_call(info, gain, own1, parts1, (late,))
    scaled1 = shared(scaled1)
    own0, *parts0 = ffn_call(info, scaled0, gain, weights)
    parts0 = exchanged(parts0)
    own1, *parts1, late = ffn_late_call(info, scaled1, gain, weights)
    parts1 = exchanged(parts1)
    result = finish_call(summed0, own0, parts0)
    return finish_call(summed1, own1, parts1, result, late)


def solution(mesh):
    inner = Mesh(mesh.devices.reshape(4, 4, 2, 4), ("x", "y", "core", "head"))
    req = ("x", "y", "core")
    in_specs = (
        P(req, "head"),
        P(req, None, "head"),
        P(req, None, None, "head"),
        P(req),
        P(req, "head"),
        P(req, None, "head"),
        P(req, None, None, "head"),
        P(req),
        P(req),
        P(req, "head"),
        P(req, "head"),
        P("head", req),
        P(),
        P(req, "head"),
        P(req, "head"),
        P("head", req),
    )
    out_specs = (P(req, "head"), P(req, "head"))

    return jax.shard_map(body, mesh=inner, in_specs=in_specs, out_specs=out_specs, check_vma=False)
```
